32 devices in a mesh: chan: 4 (over z), ctx: 8 (over y, x, core).
Axes of the slice: x: 2, y: 2, z: 4, core: 2. Of those that a mesh axis runs over, the one named last changes fastest.
Arguments:
- queries: bfloat16 [8192, 1024], P('chan', 'ctx'), may hold values from -6 to 6
- keys: bfloat16 [8192, 1024], P('chan', 'ctx'), may hold values from -6 to 6
- values: bfloat16 [8192, 1024], P('chan', 'ctx'), may hold values from -6 to 6
- out_grad: bfloat16 [1024, 8192], P('ctx', 'chan'), may hold values from -6 to 6
- out_weight: bfloat16 [8192, 8192], P('chan'), may hold values from -0.0625 to 0.0625
- residues: float32 [16, 8192], P(None, 'chan'), may hold values from -1.5 to 1.5
- decay_rates: float32 [16, 8192], P(None, 'chan'), may hold values from 0.00048828125 to 1
Outputs:
- query_grad: bfloat16 [8192, 1024], P('chan', 'ctx')
- key_grad: bfloat16 [8192, 1024], P('chan', 'ctx')
- value_grad: bfloat16 [8192, 1024], P('chan', 'ctx')
- resid_grad: float32 [16, 8192], P(None, ('chan', 'ctx'))
- decay_grad: float32 [16, 8192], P(None, ('chan', 'ctx'))
The draws below stay inside these ranges and needn't reach their ends.
All inputs are finite; a program needn't handle non-finite values.
Results may differ from the reference program's by a relative error of at most 0.0085.
Values may be sent and summed in bfloat16 or wider, within the bound.
A program may use at most 192 MiB of HBM per device.

```python
import math
import jax
import jax.numpy as jnp
from jax import lax

D = 8192
ORDER = 16
B = 1024
SEQ = 1024


def draw_queries(key, part):
    own_key = jax.random.fold_in(key, 101)
    gate_values = jnp.clip(jax.random.normal(jax.random.fold_in(own_key, 1), (D, SEQ), jnp.float32), -6.0, 6.0)
    return gate_values.astype(jnp.bfloat16)


def draw_keys(key, part):
    own_key = jax.random.fold_in(key, 102)
    gate_values = jnp.clip(jax.random.normal(jax.random.fold_in(own_key, 1), (D, SEQ), jnp.float32), -6.0, 6.0)
    return gate_values.astype(jnp.bfloat16)


def draw_values(key, part):
    own_key = jax.random.fold_in(key, 103)
    white_noise = jax.random.normal(jax.random.fold_in(own_key, 1), (D, SEQ), jnp.float32)
    return jnp.clip(white_noise, -6.0, 6.0).astype(jnp.bfloat16)


def draw_out_grad(key, part):
    own_key = jax.random.fold_in(key, 104)
    white_noise = jax.random.normal(jax.random.fold_in(own_key, 1), (SEQ, D), jnp.float32)
    return jnp.clip(white_noise, -6.0, 6.0).astype(jnp.bfloat16)


def filter_modes(key):
    mode_key = jax.random.fold_in(key, 105)
    spread = jax.random.uniform(jax.random.fold_in(mode_key, 1), (ORDER, D), jnp.float32)
    magnitude = jax.random.uniform(jax.random.fold_in(mode_key, 2), (ORDER, D), jnp.float32)
    coin_flips = jax.random.randint(jax.random.fold_in(mode_key, 3), (ORDER, D), 0, 2)
    sign_values = (1 - 2 * coin_flips).astype(jnp.float32)
    balance = jax.random.uniform(jax.random.fold_in(mode_key, 5), (ORDER, D), jnp.float32, 0.95, 1.0)
    slow_count = max(1, ORDER // 8)
    fast_count = ORDER // 4
    pair_count = (ORDER - slow_count - fast_count) // 2
    rate_rows = []
    resid_rows = []
    for slot_index in range(slow_count):
        rate_rows.append(jnp.exp(math.log(0.5) + spread[slot_index] * math.log(8.0)) / SEQ)
        resid_rows.append(sign_values[slot_index] * (0.2 + 0.4 * magnitude[slot_index]))
    for pair_index in range(pair_count):
        first_slot = slow_count + 2 * pair_index
        base_rate = jnp.exp(math.log(40.0) + spread[first_slot] * math.log(2.5)) / SEQ
        leading = jnp.minimum(base_rate, 1.0)
        trailing = jnp.minimum(0.5 * base_rate, 1.0)
        lead_resid = sign_values[first_slot] * (0.5 + 0.5 * magnitude[first_slot])
        rate_rows.append(leading)
        rate_rows.append(trailing)
        resid_rows.append(lead_resid)
        resid_rows.append(-lead_resid * jnp.sqrt(leading / trailing) * balance[first_slot])
    for slot_index in range(slow_count + 2 * pair_count, ORDER):
        rate_rows.append(jnp.minimum(jnp.exp(math.log(200.0) + spread[slot_index] * math.log(10.0)) / SEQ, 1.0))
        resid_rows.append(sign_values[slot_index] * (0.08 + 0.12 * magnitude[slot_index]))
    role_rates = jnp.stack(rate_rows)
    role_resid = jnp.stack(resid_rows)
    scores = jax.random.randint(jax.random.fold_in(mode_key, 4), (ORDER, D), 0, 1 << 20) * ORDER + jnp.arange(ORDER, dtype=jnp.int32)[:, None]
    order_index = jnp.argsort(scores, axis=0)
    return (jnp.take_along_axis(role_rates, order_index, axis=0), jnp.take_along_axis(role_resid, order_index, axis=0))


def draw_residues(key, part):
    mode_rates, mode_resid = filter_modes(key)
    return mode_resid.astype(jnp.float32)


def draw_decay_rates(key, part):
    mode_rates, mode_resid = filter_modes(key)
    return mode_rates.astype(jnp.float32)


def block_levels(key, extent, cuts, smallest, largest):
    level = 1.0
    for position, parts in cuts:
        steps = jax.random.uniform(jax.random.fold_in(jax.random.fold_in(key, 6), position), (parts,), jnp.float32, smallest / len(cuts), largest / len(cuts))
        level = level * jnp.repeat(jnp.exp(steps), extent[position] // parts).reshape((-1,) + (1,) * (len(extent) - 1 - position))
    return level


def noise(key, shape, scale, reach, shards=(), kind=jnp.bfloat16):
    loudness = block_levels(key, shape, shards, -0.22, 0.18) if shards else 1.0
    entries = jax.random.normal(key, shape, jnp.float32) * scale * loudness
    return jnp.minimum(jnp.maximum(entries, -reach), reach).astype(kind)


def setup_inputs(seed: int = 0) -> dict:
    seeds = jax.random.split(jax.random.key(seed), 8)
    return {
        "queries": draw_queries(jax.random.fold_in(seeds[7], 71), 0),
        "keys": draw_keys(jax.random.fold_in(seeds[7], 71), 0),
        "values": draw_values(jax.random.fold_in(seeds[7], 71), 0),
        "out_grad": draw_out_grad(jax.random.fold_in(seeds[7], 71), 0),
        "out_weight": noise(seeds[4], (D, D), D ** -0.5, 0.0625, ((0, 4),)),
        "residues": draw_residues(jax.random.fold_in(seeds[7], 71), 0),
        "decay_rates": draw_decay_rates(jax.random.fold_in(seeds[7], 71), 0),
    }


PRECISE = lax.Precision.HIGHEST

def dft_tables(block_size, section_size):
    total_size = section_size * block_size
    inner = jnp.arange(block_size, dtype=jnp.int32)
    outer = jnp.arange(section_size, dtype=jnp.int32)
    half_size = section_size // 2
    inner_angle = (inner[:, None] * inner[None, :] % block_size).astype(jnp.float32) * (2.0 * math.pi / block_size)
    twist_angle = (outer[:, None] * inner[None, :] % total_size).astype(jnp.float32) * (2.0 * math.pi / total_size)
    outer_rows = jnp.arange(half_size, dtype=jnp.int32)
    outer_angle = (outer_rows[:, None] * outer[None, :] % section_size).astype(jnp.float32) * (2.0 * math.pi / section_size)
    return (jnp.cos(inner_angle).astype(jnp.bfloat16), jnp.sin(inner_angle).astype(jnp.bfloat16), jnp.cos(twist_angle), jnp.sin(twist_angle), jnp.cos(outer_angle).astype(jnp.bfloat16), jnp.sin(outer_angle).astype(jnp.bfloat16))

def forward(signal, tables):
    big_cos, big_sin, twist_cos, twist_sin, small_cos, small_sin = tables
    channels = signal.shape[0]
    half_size, section_size = small_cos.shape
    block_size = big_cos.shape[0]
    grid_view = signal.astype(jnp.float32).reshape(channels, half_size, block_size)
    outer_cos = small_cos.astype(jnp.float32)
    outer_sin = small_sin.astype(jnp.float32)
    real_part = jnp.einsum('chb,hk->ckb', grid_view, outer_cos, precision=PRECISE)
    imag_part = -jnp.einsum('chb,hk->ckb', grid_view, outer_sin, precision=PRECISE)
    turned_re = (real_part * twist_cos + imag_part * twist_sin).astype(jnp.bfloat16).reshape(channels * section_size, block_size)
    turned_im = (imag_part * twist_cos - real_part * twist_sin).astype(jnp.bfloat16).reshape(channels * section_size, block_size)
    out_re = jnp.dot(turned_re, big_cos, preferred_element_type=jnp.float32) + jnp.dot(turned_im, big_sin, preferred_element_type=jnp.float32)
    out_im = jnp.dot(turned_im, big_cos, preferred_element_type=jnp.float32) - jnp.dot(turned_re, big_sin, preferred_element_type=jnp.float32)
    return (out_re.reshape(channels, section_size, block_size), out_im.reshape(channels, section_size, block_size))

def inverse(spec_re, spec_im, tables):
    big_cos, big_sin, twist_cos, twist_sin, small_cos, small_sin = tables
    channels, section_size, block_size = spec_re.shape
    half_size = small_cos.shape[0]
    flat_re = spec_re.astype(jnp.bfloat16).reshape(channels * section_size, block_size)
    flat_im = spec_im.astype(jnp.bfloat16).reshape(channels * section_size, block_size)
    back_re = jnp.dot(flat_re, big_cos, preferred_element_type=jnp.float32) - jnp.dot(flat_im, big_sin, preferred_element_type=jnp.float32)
    back_im = jnp.dot(flat_re, big_sin, preferred_element_type=jnp.float32) + jnp.dot(flat_im, big_cos, preferred_element_type=jnp.float32)
    back_re = back_re.reshape(channels, section_size, block_size)
    back_im = back_im.reshape(channels, section_size, block_size)
    wound_re = lax.optimization_barrier((back_re * twist_cos - back_im * twist_sin).astype(jnp.bfloat16)).astype(jnp.float32)
    wound_im = lax.optimization_barrier((back_re * twist_sin + back_im * twist_cos).astype(jnp.bfloat16)).astype(jnp.float32)
    outer_cos = small_cos.astype(jnp.float32)
    outer_sin = small_sin.astype(jnp.float32)
    grid_view = jnp.einsum('ckb,hk->chb', wound_re, outer_cos, precision=PRECISE) - jnp.einsum('ckb,hk->chb', wound_im, outer_sin, precision=PRECISE)
    return grid_view.reshape(channels, half_size * block_size) * (1.0 / (section_size * block_size))

def filter_spectrum(resid, rates, tables):
    small_cos = tables[4]
    section_size = small_cos.shape[1]
    block_size = tables[0].shape[0]
    total_size = section_size * block_size
    seq_length = total_size // 2
    frequency = jnp.arange(section_size, dtype=jnp.int32)[:, None] + section_size * jnp.arange(block_size, dtype=jnp.int32)[None, :]
    half_angle = frequency.astype(jnp.float32) * (math.pi / total_size)
    sine_half = jnp.sin(half_angle)
    sine_square = sine_half * sine_half
    sine_full = jnp.sin(2.0 * half_angle)
    parity = 1.0 - 2.0 * (frequency % 2).astype(jnp.float32)

    def add_mode(running, mode_vals):
        decay_rate, amplitude = mode_vals
        ratio = jnp.exp(-decay_rate)[:, None, None]
        one_minus = (-jnp.expm1(-decay_rate))[:, None, None]
        tail_value = jnp.exp(-decay_rate * seq_length)[:, None, None]
        root_gain = (amplitude * jnp.sqrt(2.0 * decay_rate))[:, None, None]
        den_real = one_minus + 2.0 * ratio * sine_square
        den_imag = ratio * sine_full
        modulus = one_minus * one_minus + 4.0 * ratio * sine_square
        numerator = root_gain * (1.0 - tail_value * parity) / modulus
        return ((running[0] + numerator * den_real, running[1] - numerator * den_imag), None)
    channels = resid.shape[1]
    initial = (jnp.zeros((channels, section_size, block_size), jnp.float32), jnp.zeros((channels, section_size, block_size), jnp.float32))
    result, unused = lax.scan(add_mode, initial, (rates, resid))
    return result

def filter_grads(kernel_grad, resid, rates):
    positions = jnp.arange(kernel_grad.shape[1], dtype=jnp.int32).astype(jnp.float32)

    def one_mode(unused_carry, mode_vals):
        decay_rate, amplitude = mode_vals
        decay_curve = jnp.exp(-decay_rate[:, None] * positions[None, :])
        weighted = kernel_grad * decay_curve
        plain_sum = lax.optimization_barrier(jnp.sum(weighted, axis=1))
        moment_sum = lax.optimization_barrier(jnp.sum(weighted * positions[None, :], axis=1))
        root_gain = jnp.sqrt(2.0 * decay_rate)
        return (unused_carry, (root_gain * plain_sum, amplitude * root_gain * (0.5 * plain_sum - decay_rate * moment_sum)))
    unused, grads = lax.scan(one_mode, jnp.zeros((), jnp.float32), (rates, resid))
    return grads

def conv_core(product, conv_grad, resid, rates, tables):
    spec_re, spec_im = filter_spectrum(resid, rates, tables)
    src_re, src_im = forward(product, tables)
    drv_re, drv_im = forward(conv_grad, tables)
    conv_out = inverse(spec_re * src_re - spec_im * src_im, spec_re * src_im + spec_im * src_re, tables).astype(jnp.bfloat16)
    product_grad = inverse(spec_re * drv_re + spec_im * drv_im, spec_re * drv_im - spec_im * drv_re, tables).astype(jnp.bfloat16)
    kernel_grad = inverse(drv_re * src_re + drv_im * src_im, drv_im * src_re - drv_re * src_im, tables)
    resid_grad, decay_grad = filter_grads(kernel_grad, resid, rates)
    return (conv_out, product_grad, resid_grad, decay_grad)

def reference(queries, keys, values, out_grad, out_weight, residues, decay_rates):
    channels, seq_length = queries.shape
    section_size = 2 * seq_length // B
    tables = dft_tables(B, section_size)
    mixer_grad = jnp.dot(out_weight, out_grad.T, preferred_element_type=jnp.float32).astype(jnp.bfloat16)
    group_width = 64
    block_count = channels // group_width

    def one_block(block_index):
        first_row = block_index * group_width
        query_rows = lax.dynamic_slice_in_dim(queries, first_row, group_width, 0)
        key_rows = lax.dynamic_slice_in_dim(keys, first_row, group_width, 0)
        value_rows = lax.dynamic_slice_in_dim(values, first_row, group_width, 0)
        mixer_rows = lax.dynamic_slice_in_dim(mixer_grad, first_row, group_width, 0)
        resid = lax.dynamic_slice_in_dim(residues, first_row, group_width, 1)
        rates = lax.dynamic_slice_in_dim(decay_rates, first_row, group_width, 1)
        product = (key_rows.astype(jnp.float32) * value_rows.astype(jnp.float32)).astype(jnp.bfloat16)
        conv_grad = (mixer_rows.astype(jnp.float32) * query_rows.astype(jnp.float32)).astype(jnp.bfloat16)
        conv_out, product_grad, resid_grad, decay_grad = conv_core(product, conv_grad, resid, rates, tables)
        query_grad = (mixer_rows.astype(jnp.float32) * conv_out.astype(jnp.float32)).astype(jnp.bfloat16)
        key_grad = (product_grad.astype(jnp.float32) * value_rows.astype(jnp.float32)).astype(jnp.bfloat16)
        value_grad = (product_grad.astype(jnp.float32) * key_rows.astype(jnp.float32)).astype(jnp.bfloat16)
        return (query_grad, key_grad, value_grad, resid_grad, decay_grad)
    query_grad, key_grad, value_grad, resid_grad, decay_grad = lax.map(one_block, jnp.arange(block_count, dtype=jnp.int32))
    order_count = residues.shape[0]
    return (query_grad.reshape(channels, seq_length), key_grad.reshape(channels, seq_length), value_grad.reshape(channels, seq_length), jnp.transpose(resid_grad, (1, 0, 2)).reshape(order_count, channels), jnp.transpose(decay_grad, (1, 0, 2)).reshape(order_count, channels))
```

```python
import functools

import jax
import jax.numpy as jnp
from jax import lax
from jax.experimental import pallas as pl
from jax.experimental.pallas import tpu as pltpu
from jax.sharding import PartitionSpec as P

STEP = 16
LANES = 128
HALVES = 2
SPLITS = 2
MESH = pl.DeviceIdType.MESH
F32, BF16 = jnp.float32, jnp.bfloat16


def fold_rows(rows):
    lanes = rows[0].shape[1]
    sub = lax.broadcasted_iota(jnp.int32, (8, lanes), 0)
    low4, low2, low1 = sub < 4, (sub & 2) == 0, (sub & 1) == 0
    four = []
    for i in range(4):
        a, b = rows[i], rows[i + 4]
        four.append(jnp.where(low4, a, b) + pltpu.roll(jnp.where(low4, b, a), 4, 0))
    two = []
    for i in range(2):
        a, b = four[i], four[i + 2]
        two.append(
            jnp.where(low2, a, pltpu.roll(b, 2, 0)) + jnp.where(low2, pltpu.roll(a, 6, 0), b)
        )
    a, b = two
    return jnp.where(low1, a, pltpu.roll(b, 1, 0)) + jnp.where(low1, pltpu.roll(a, 7, 0), b)


def fold_block(totals):
    return jnp.concatenate([fold_rows(totals[i : i + 8]) for i in range(0, STEP, 8)], axis=0)


def rounded(x):
    return x.astype(BF16).astype(F32)


def tree_sum(terms):
    while len(terms) > 1:
        terms = [a + b for a, b in zip(terms[::2], terms[1::2])] + (
            [terms[-1]] if len(terms) % 2 else []
        )
    return terms[0]


def body(
    chan_size,
    ctx_size,
    queries,
    keys,
    values,
    out_grad,
    out_weight,
    residues,
    decay_rates,
    own_residues,
    own_rates,
    query_grad,
    key_grad,
    value_grad,
    resid_grad,
    decay_grad,
    weight,
    gathered,
    source,
    gate,
    mixer,
    drive,
    conv,
    adjoint,
    powers,
    decay,
    gain,
    decay_eight,
    held_now,
    causal_start,
    plain_sum,
    moment_sum,
    causal_end_out,
    causal_end_in,
    causal_in_out,
    causal_in_in,
    end_out,
    end_in,
    start_out,
    start_in,
    sums_out,
    sums_in,
    weight_sems,
    shard_arrivals,
    up_sends,
    down_sends,
    sends,
    arrivals,
):
    place = lax.axis_index("chan")
    me = lax.axis_index("ctx")
    channels, tokens = queries.shape
    depth = out_grad.shape[1]
    width = channels // ctx_size
    order = residues.shape[0]
    count = order // 8
    half = tokens // HALVES
    piece = depth // SPLITS
    own = slice(None)
    if own_rates.shape[1] != width:
        own = pl.ds(pl.multiple_of(me * width, width), width)
    tile = min(channels, 512)

    def links(kind, outgoing, incoming):
        return (outgoing, incoming, sends.at[kind], arrivals.at[kind])

    causal_end_links = links(0, causal_end_out, causal_end_in)
    causal_in_links = links(1, causal_in_out, causal_in_in)
    end_links = links(2, end_out, end_in)
    start_links = links(3, start_out, start_in)
    sums_links = links(4, sums_out, sums_in)

    def exchange(link, other):
        outgoing, incoming, sent, arrived = link
        return pltpu.make_async_remote_copy(
            src_ref=outgoing.at[other],
            dst_ref=incoming.at[me],
            send_sem=sent.at[other],
            recv_sem=arrived.at[me],
            device_id={"ctx": other},
            device_id_type=MESH,
        )

    def send_or_keep(link, other):
        @pl.when(other != me)
        def _():
            exchange(link, other).start()

        @pl.when(other == me)
        def _():
            link[1][me] = link[0][me]

    def await_slot(link, other):
        outgoing, incoming, sent, arrived = link

        @pl.when(other != me)
        def _():
            pltpu.make_async_remote_copy(
                src_ref=outgoing.at[other],
                dst_ref=incoming.at[other],
                send_sem=sent.at[other],
                recv_sem=arrived.at[other],
                device_id={"ctx": other},
                device_id_type=MESH,
            ).wait_recv()

    def send_all(link):
        @pl.loop(0, ctx_size)
        def _(step):
            send_or_keep(link, lax.rem(me + 1 + step, ctx_size))

    def weight_copy(shard):
        return pltpu.make_async_copy(
            out_weight.at[:, pl.ds(pl.multiple_of(shard * depth, depth), depth)],
            weight.at[shard],
            weight_sems.at[shard],
        )

    parts = [(h, e) for h in reversed(range(HALVES)) for e in range(SPLITS)]

    def shard_copy(shard, part, going_up, first=False):
        h, e = parts[part]
        rows, cols = pl.ds(h * half, half), pl.ds(e * piece, piece)
        return pltpu.make_async_remote_copy(
            src_ref=out_grad.at[rows, cols] if first else gathered.at[shard, e, rows],
            dst_ref=gathered.at[shard, e, rows],
            send_sem=(up_sends if going_up else down_sends).at[shard, part],
            recv_sem=shard_arrivals.at[shard, part],
            device_id={"chan": place + 1 if going_up else place - 1},
            device_id_type=MESH,
        )

    weight_copy(place).start()
    for distance in range(1, chan_size):
        for shard, present in (
            (place - distance, place >= distance),
            (place + distance, place + distance < chan_size),
        ):

            @pl.when(present)
            def _():
                weight_copy(shard).start()

    barrier = pltpu.get_barrier_semaphore()
    for step in range(1, ctx_size):
        pl.semaphore_signal(
            barrier, inc=1, device_id={"ctx": lax.rem(me + step, ctx_size)}, device_id_type=MESH
        )
    for present, neighbour in ((place > 0, place - 1), (place < chan_size - 1, place + 1)):

        @pl.when(present)
        def _():
            pl.semaphore_signal(
                barrier, inc=1, device_id={"chan": neighbour}, device_id_type=MESH
            )

    sides = jnp.where(place > 0, 1, 0) + jnp.where(place < chan_size - 1, 1, 0)
    pl.semaphore_wait(barrier, ctx_size - 1 + sides)

    for part in range(len(parts)):

        @pl.when(place < chan_size - 1)
        def _():
            shard_copy(place, part, True, True).start()

        @pl.when(place > 0)
        def _():
            shard_copy(place, part, False, True).start()

    rate = decay_rates[...]
    decay[...] = jnp.exp(-rate)
    gain[...] = residues[...] * jnp.sqrt(2.0 * rate)
    decay_eight[...] = jnp.exp(-8.0 * rate)

    @pl.loop(0, channels // LANES)
    def _(index):
        cols = pl.ds(pl.multiple_of(index * LANES, LANES), LANES)
        pair = keys[cols, :].astype(F32) * values[cols, :].astype(F32)
        source[:, cols] = rounded(pair).T
        gate[:, cols] = queries[cols, :].astype(F32).T

    def spread(row):
        return jnp.broadcast_to(row, (8, LANES))

    def column(group, number, position):
        return pl.ds(pl.multiple_of((group * number + position) * LANES, LANES), LANES)

    def modes_of(table, cols):
        return [table[8 * g : 8 * g + 8, cols] for g in range(count)]

    wide = 4 if channels % (4 * LANES) == 0 else 1

    @pl.loop(0, channels // (wide * LANES))
    def _(group):
        columns = [column(group, wide, position) for position in range(wide)]
        modes = [modes_of(decay, cols) for cols in columns]

        def block(index, state):
            base = pl.multiple_of(index * STEP, STEP)
            state = [[list(pair) for pair in entry] for entry in state]
            for position, cols in enumerate(columns):
                rows = source[pl.ds(base, STEP), cols]
                for step in range(STEP):
                    row = spread(rows[step : step + 1, :])
                    for g in range(count):
                        held, moment = state[position][g]
                        factor = modes[position][g]
                        state[position][g] = [factor * held + row, factor * (moment + held)]
            return tuple(tuple(tuple(pair) for pair in entry) for entry in state)

        zero = jnp.zeros((8, LANES), F32)
        state = lax.fori_loop(
            0, tokens // STEP, block, (((zero, zero),) * count,) * wide
        )
        for position, cols in enumerate(columns):
            for g in range(count):
                plain_sum[8 * g : 8 * g + 8, cols] = state[position][g][0]
                moment_sum[8 * g : 8 * g + 8, cols] = state[position][g][1]

    for other in range(ctx_size):
        cols = slice(other * width, (other + 1) * width)
        causal_end_out[other, 0] = plain_sum[:, cols]
        causal_end_out[other, 1] = moment_sum[:, cols]
    send_all(causal_end_links)

    plain_sum[...] = jnp.zeros((order, channels), F32)
    moment_sum[...] = jnp.zeros((order, channels), F32)
    held_now[...] = jnp.zeros((order, channels), F32)

    def multiply(lefts, shard, rows, first=False):
        @pl.loop(0, channels // tile)
        def _(index):
            cols = pl.ds(pl.multiple_of(index * tile, tile), tile)
            term = tree_sum(
                [
                    lax.dot_general(
                        left[...],
                        weight[shard, cols, taken],
                        (((1,), (1,)), ((), ())),
                        preferred_element_type=F32,
                    )
                    for left, taken in lefts
                ]
            )
            mixer[rows, cols] = term if first else mixer[rows, cols] + term

    everything = slice(None)
    weight_copy(place).wait()
    multiply([(out_grad, everything)], place, everything, True)

    def around(distance):
        return (
            (place - distance, place >= distance, place < chan_size - 1, True),
            (place + distance, place + distance < chan_size, place > 0, False),
        )

    def relay(distance):
        for part in range(len(parts)):
            for shard, present, onward, going_up in around(distance):

                @pl.when(present)
                def _():
                    shard_copy(shard, part, going_up).wait_recv()

                    @pl.when(onward)
                    def _():
                        shard_copy(shard, part, going_up).start()

    def take_whole(distance):
        for shard, present, onward, going_up in around(distance):

            @pl.when(present)
            def _():
                weight_copy(shard).wait()
                multiply(
                    [
                        (gathered.at[shard, e], pl.ds(e * piece, piece))
                        for e in range(SPLITS)
                    ],
                    shard,
                    everything,
                )

    own_rate = own_rates[:, own]
    own_far = jnp.exp(-own_rate * tokens)

    def causal_states():
        held = jnp.zeros((order, width), F32)
        moment = jnp.zeros((order, width), F32)
        for block in range(ctx_size):
            causal_in_out[block, 0] = held
            causal_in_out[block, 1] = moment
            if block < ctx_size - 1:
                await_slot(causal_end_links, block)
                moment = causal_end_in[block, 1] + own_far * (moment + float(tokens) * held)
                held = causal_end_in[block, 0] + own_far * held
        await_slot(causal_end_links, ctx_size - 1)
        send_all(causal_in_links)

    double = 2 if channels % (2 * LANES) == 0 else 1

    def causal_scan():
        for other in range(ctx_size):
            await_slot(causal_in_links, other)
            cols = slice(other * width, (other + 1) * width)
            causal_start[0, 0, :, cols] = causal_in_in[other, 0]
            causal_start[0, 1, :, cols] = causal_in_in[other, 1]

        @pl.loop(0, channels // (double * LANES))
        def _(group):
            columns = [column(group, double, position) for position in range(double)]
            factors = [modes_of(decay, cols) for cols in columns]
            gains = [modes_of(gain, cols) for cols in columns]

            def block(index, state):
                base = pl.multiple_of(index * STEP, STEP)
                state = [[list(pair) for pair in entry] for entry in state]
                for position, cols in enumerate(columns):
                    rows = source[pl.ds(base, STEP), cols]
                    totals = []
                    for step in range(STEP):
                        row = spread(rows[step : step + 1, :])
                        terms = []
                        for g in range(count):
                            held, moment = state[position][g]
                            factor = factors[position][g]
                            moment = factor * (moment + held)
                            held = factor * held + row
                            state[position][g] = [held, moment]
                            terms.append(gains[position][g] * held)
                        totals.append(tree_sum(terms))
                    conv[pl.ds(base, STEP), cols] = rounded(fold_block(totals))
                return tuple(tuple(tuple(pair) for pair in entry) for entry in state)

            state = tuple(
                tuple(
                    (
                        causal_start[0, 0, 8 * g : 8 * g + 8, cols],
                        causal_start[0, 1, 8 * g : 8 * g + 8, cols],
                    )
                    for g in range(count)
                )
                for cols in columns
            )
            steps = half // STEP
            for h in range(HALVES):
                if h:
                    for position, cols in enumerate(columns):
                        for g in range(count):
                            for kind in range(2):
                                causal_start[h, kind, 8 * g : 8 * g + 8, cols] = state[position][g][kind]
                state = lax.fori_loop(h * steps, (h + 1) * steps, block, state)

    def power_table():
        sub = lax.broadcasted_iota(jnp.int32, (8, LANES), 0).astype(F32)

        @pl.loop(0, channels // LANES)
        def _(index):
            cols = pl.ds(pl.multiple_of(index * LANES, LANES), LANES)
            for n in range(order):
                table = jnp.exp(-spread(decay_rates[n : n + 1, cols]) * (8.0 - sub))
                powers[n, :, cols] = table * spread(gain[n : n + 1, cols])

    def adjoint_scan(h):
        @pl.loop(0, channels // (double * LANES))
        def _(group):
            columns = [column(group, double, position) for position in range(double)]
            factors = [modes_of(decay, cols) for cols in columns]
            gains = [modes_of(gain, cols) for cols in columns]
            steps = half // STEP

            def block(index, state):
                base = pl.multiple_of(h * half + (steps - 1 - index) * STEP, STEP)
                state = [list(entry) for entry in state]
                for position, cols in enumerate(columns):
                    where = (pl.ds(base, STEP), cols)
                    rows = rounded(rounded(mixer[where]) * gate[where])
                    drive[where] = rows
                    totals = [None] * STEP
                    for step in reversed(range(STEP)):
                        row = spread(rows[step : step + 1, :])
                        terms = []
                        for g in range(count):
                            held = factors[position][g] * state[position][g] + row
                            state[position][g] = held
                            terms.append(gains[position][g] * held)
                        totals[step] = tree_sum(terms)
                    adjoint[where] = fold_block(totals)
                return tuple(tuple(entry) for entry in state)

            state = lax.fori_loop(
                0, steps, block, tuple(tuple(modes_of(held_now, cols)) for cols in columns)
            )
            for position, cols in enumerate(columns):
                for g in range(count):
                    held_now[8 * g : 8 * g + 8, cols] = state[position][g]

    def sum_scan(h):
        @pl.loop(0, channels // (double * LANES))
        def _(group):
            columns = [column(group, double, position) for position in range(double)]
            factors = [modes_of(decay, cols) for cols in columns]
            steps = half // STEP

            def block(index, state):
                base = pl.multiple_of(h * half + index * STEP, STEP)
                state = [[list(item) for item in entry] for entry in state]
                for position, cols in enumerate(columns):
                    where = (pl.ds(base, STEP), cols)
                    rows, drives = source[where], drive[where]
                    for step in range(STEP):
                        row = spread(rows[step : step + 1, :])
                        push = spread(drives[step : step + 1, :])
                        for g in range(count):
                            held, moment, plain, slope = state[position][g]
                            factor = factors[position][g]
                            moment = factor * (moment + held)
                            held = factor * held + row
                            state[position][g] = [
                                held,
                                moment,
                                plain + push * held,
                                slope + push * moment,
                            ]
                return tuple(tuple(tuple(item) for item in entry) for entry in state)

            state = tuple(
                tuple(
                    (
                        causal_start[h, 0, 8 * g : 8 * g + 8, cols],
                        causal_start[h, 1, 8 * g : 8 * g + 8, cols],
                        plain_sum[8 * g : 8 * g + 8, cols],
                        moment_sum[8 * g : 8 * g + 8, cols],
                    )
                    for g in range(count)
                )
                for cols in columns
            )
            state = lax.fori_loop(0, steps, block, state)
            for position, cols in enumerate(columns):
                for g in range(count):
                    plain_sum[8 * g : 8 * g + 8, cols] = state[position][g][2]
                    moment_sum[8 * g : 8 * g + 8, cols] = state[position][g][3]

    if chan_size > 2:
        relay(1)
    causal_states()
    if chan_size > 2:
        take_whole(1)
    causal_scan()
    power_table()
    for distance in range(2, chan_size - 1):
        relay(distance)
        take_whole(distance)

    last = jnp.where(place == 0, chan_size - 1, 0)
    at_end = (place == 0) | (place == chan_size - 1)

    if chan_size > 1:

        @pl.when(at_end)
        def _():
            weight_copy(last).wait()

    for h in reversed(range(HALVES)):
        if chan_size > 1:
            for part, (number, e) in enumerate(parts):
                if number == h:

                    @pl.when(at_end)
                    def _():
                        rows = pl.ds(h * half, half)
                        shard_copy(last, part, True).wait_recv()
                        multiply(
                            [(gathered.at[last, e, rows], pl.ds(e * piece, piece))], last, rows
                        )

        adjoint_scan(h)
        if h:
            sum_scan(h)

    for other in range(ctx_size):
        end_out[other] = held_now[:, other * width : (other + 1) * width]
    send_all(end_links)
    sum_scan(0)
    for other in range(ctx_size):
        cols = slice(other * width, (other + 1) * width)
        sums_out[other, 0] = plain_sum[:, cols]
        sums_out[other, 1] = moment_sum[:, cols]

    held = jnp.zeros((order, width), F32)
    for block in reversed(range(ctx_size)):
        start_out[block] = held
        send_or_keep(start_links, block)
        await_slot(end_links, block)
        if block:
            held = end_in[block] + own_far * held
    send_all(sums_links)

    @pl.loop(0, channels // LANES)
    def _(index):
        cols = pl.ds(pl.multiple_of(index * LANES, LANES), LANES)
        query_grad[cols, :] = (rounded(mixer[:, cols]) * conv[:, cols]).T.astype(BF16)

    for other in range(ctx_size):
        await_slot(start_links, other)
        held_now[:, other * width : (other + 1) * width] = start_in[other]

    @pl.loop(0, channels // LANES)
    def _(index):
        cols = pl.ds(pl.multiple_of(index * LANES, LANES), LANES)
        terms = [powers[n, :, cols] * spread(held_now[n : n + 1, cols]) for n in range(order)]
        factors = [spread(decay_eight[n : n + 1, cols]) for n in range(order)]
        pieces = [None] * (tokens // 8)
        for group in reversed(range(tokens // 8)):
            pieces[group] = adjoint[8 * group : 8 * group + 8, cols] + tree_sum(list(terms))
            if group:
                terms = [term * factor for term, factor in zip(terms, factors)]
        result = rounded(jnp.concatenate(pieces, axis=0)).T
        key_grad[cols, :] = (result * values[cols, :].astype(F32)).astype(BF16)
        value_grad[cols, :] = (result * keys[cols, :].astype(F32)).astype(BF16)

    plain = jnp.zeros((order, width), F32)
    slope = jnp.zeros((order, width), F32)
    for other in range(ctx_size):
        await_slot(sums_links, other)
        plain = plain + sums_in[other, 0]
        slope = slope + sums_in[other, 1]
    root = jnp.sqrt(2.0 * own_rate)
    resid_grad[...] = root * plain
    decay_grad[...] = own_residues[:, own] * root * (0.5 * plain - own_rate * slope)

    @pl.loop(0, ctx_size)
    def _(other):
        @pl.when(other != me)
        def _():
            for link in (causal_end_links, causal_in_links, end_links, start_links, sums_links):
                exchange(link, other).wait_send()

    for distance in range(chan_size - 1):
        for shard, present, onward, going_up in around(distance):

            @pl.when(present & onward)
            def _():
                for part in range(len(parts)):
                    shard_copy(shard, part, going_up, distance == 0).wait_send()


def hand_over(*refs):
    number = len(refs) // 2
    copies = [
        pltpu.make_async_copy(refs[i], refs[number + i], refs[-1].at[i]) for i in range(number)
    ]
    for copy in copies:
        copy.start()
    for copy in copies:
        copy.wait()


def local(queries, keys, values, out_grad, out_weight, residues, decay_rates):
    channels, tokens = queries.shape
    chan_size = lax.axis_size("chan")
    ctx_size = lax.axis_size("ctx")
    width = channels // ctx_size
    depth = out_grad.shape[1]
    order = residues.shape[0]
    owned = residues, decay_rates
    if width % LANES:
        offset = lax.axis_index("ctx") * width
        owned = [lax.dynamic_slice_in_dim(x, offset, width, 1) for x in owned]
    number = HALVES * SPLITS
    gate = jax.ShapeDtypeStruct((channels, tokens), BF16)
    grads = jax.ShapeDtypeStruct((order, width), F32)
    shapes = (gate,) * 3 + (grads,) * 2
    vmem = pl.BlockSpec(memory_space=pltpu.VMEM)
    anywhere = pl.BlockSpec(memory_space=pl.ANY)
    dma = pltpu.SemaphoreType.DMA
    plane = pltpu.VMEM((tokens, channels), F32)
    table = pltpu.VMEM((order, channels), F32)
    single = pltpu.VMEM((ctx_size, order, width), F32)
    twice = pltpu.VMEM((ctx_size, 2, order, width), F32)
    results = pl.pallas_call(
        functools.partial(body, chan_size, ctx_size),
        out_shape=shapes,
        in_specs=[vmem, vmem, vmem, vmem, anywhere, vmem, vmem, vmem, vmem],
        out_specs=(vmem,) * 5,
        scratch_shapes=[
            pltpu.VMEM((chan_size, channels, depth), BF16),
            pltpu.VMEM((chan_size, SPLITS, tokens, depth // SPLITS), BF16),
            *[plane] * 6,
            pltpu.VMEM((order, 8, channels), F32),
            *[table] * 4,
            pltpu.VMEM((HALVES, 2, order, channels), F32),
            *[table] * 2,
            *[twice] * 4,
            *[single] * 4,
            *[twice] * 2,
            dma((chan_size,)),
            dma((chan_size, number)),
            dma((chan_size, number)),
            dma((chan_size, number)),
            dma((5, ctx_size)),
            dma((5, ctx_size)),
        ],
        compiler_params=pltpu.CompilerParams(
            collective_id=0, has_side_effects=True, vmem_limit_bytes=52 * 1024 * 1024
        ),
    )(queries, keys, values, out_grad, out_weight, residues, decay_rates, *owned)
    return pl.pallas_call(
        hand_over,
        out_shape=shapes,
        in_specs=[vmem] * 5,
        out_specs=(anywhere,) * 5,
        scratch_shapes=[dma((5,))],
    )(*results)


def solution(mesh):
    placed = (
        P("chan", "ctx"),
        P("chan", "ctx"),
        P("chan", "ctx"),
        P("ctx", "chan"),
        P("chan", None),
        P(None, "chan"),
        P(None, "chan"),
    )
    return jax.shard_map(
        local,
        mesh=mesh,
        in_specs=placed,
        out_specs=(
            P("chan", "ctx"),
            P("chan", "ctx"),
            P("chan", "ctx"),
            P(None, ("chan", "ctx")),
            P(None, ("chan", "ctx")),
        ),
        check_vma=False,
    )
```

```python
import functools

import jax
import jax.numpy as jnp
from jax import lax
from jax.experimental import pallas as pl
from jax.experimental.pallas import tpu as pltpu
from jax.sharding import PartitionSpec as P

STEP = 8
SUB = 8
LANES = 128
HALVES = 2
SPLITS = 2
MESH = pl.DeviceIdType.MESH
F32, BF16 = jnp.float32, jnp.bfloat16


def rounded(x):
    return x.astype(BF16).astype(F32)


def tree_sum(terms):
    while len(terms) > 1:
        terms = [a + b for a, b in zip(terms[::2], terms[1::2])] + (
            [terms[-1]] if len(terms) % 2 else []
        )
    return terms[0]


def body(
    chan_size,
    ctx_size,
    queries,
    keys,
    values,
    out_grad,
    out_weight,
    residues,
    decay_rates,
    own_residues,
    own_rates,
    query_grad,
    key_grad,
    value_grad,
    resid_grad,
    decay_grad,
    weight,
    gathered,
    gate,
    mixer,
    source,
    drive,
    conv,
    adjoint,
    decay,
    gain,
    held_now,
    plain_sum,
    moment_sum,
    starts,
    incoming,
    causal_end_out,
    causal_end_in,
    causal_in_out,
    causal_in_in,
    end_out,
    end_in,
    start_out,
    start_in,
    sums_out,
    sums_in,
    weight_sems,
    shard_arrivals,
    up_sends,
    down_sends,
    sends,
    arrivals,
):
    place = lax.axis_index("chan")
    me = lax.axis_index("ctx")
    channels, tokens = queries.shape
    depth = out_grad.shape[1]
    width = channels // ctx_size
    order = residues.shape[0]
    count = order // 8
    half = tokens // HALVES
    piece = depth // SPLITS
    own = slice(None)
    if own_rates.shape[1] != width:
        own = pl.ds(pl.multiple_of(me * width, width), width)
    tile = min(channels, 512)

    def links(kind, outgoing, incoming):
        return (outgoing, incoming, sends.at[kind], arrivals.at[kind])

    causal_end_links = links(0, causal_end_out, causal_end_in)
    causal_in_links = links(1, causal_in_out, causal_in_in)
    end_links = links(2, end_out, end_in)
    start_links = links(3, start_out, start_in)
    sums_links = links(4, sums_out, sums_in)

    def exchange(link, other):
        outgoing, incoming, sent, arrived = link
        return pltpu.make_async_remote_copy(
            src_ref=outgoing.at[other],
            dst_ref=incoming.at[me],
            send_sem=sent.at[other],
            recv_sem=arrived.at[me],
            device_id={"ctx": other},
            device_id_type=MESH,
        )

    def send_or_keep(link, other):
        @pl.when(other != me)
        def _():
            exchange(link, other).start()

        @pl.when(other == me)
        def _():
            link[1][me] = link[0][me]

    def await_slot(link, other):
        outgoing, incoming, sent, arrived = link

        @pl.when(other != me)
        def _():
            pltpu.make_async_remote_copy(
                src_ref=outgoing.at[other],
                dst_ref=incoming.at[other],
                send_sem=sent.at[other],
                recv_sem=arrived.at[other],
                device_id={"ctx": other},
                device_id_type=MESH,
            ).wait_recv()

    def send_all(link):
        @pl.loop(0, ctx_size)
        def _(step):
            send_or_keep(link, lax.rem(me + 1 + step, ctx_size))

    def weight_copy(shard):
        return pltpu.make_async_copy(
            out_weight.at[:, pl.ds(pl.multiple_of(shard * depth, depth), depth)],
            weight.at[shard],
            weight_sems.at[shard],
        )

    parts = [(h, e) for h in reversed(range(HALVES)) for e in range(SPLITS)]

    def shard_copy(shard, part, going_up, first=False):
        h, e = parts[part]
        rows, cols = pl.ds(h * half, half), pl.ds(e * piece, piece)
        return pltpu.make_async_remote_copy(
            src_ref=out_grad.at[rows, cols] if first else gathered.at[shard, e, rows],
            dst_ref=gathered.at[shard, e, rows],
            send_sem=(up_sends if going_up else down_sends).at[shard, part],
            recv_sem=shard_arrivals.at[shard, part],
            device_id={"chan": place + 1 if going_up else place - 1},
            device_id_type=MESH,
        )

    weight_copy(place).start()
    for distance in range(1, chan_size):
        for shard, present in (
            (place - distance, place >= distance),
            (place + distance, place + distance < chan_size),
        ):

            @pl.when(present)
            def _():
                weight_copy(shard).start()

    barrier = pltpu.get_barrier_semaphore()
    for step in range(1, ctx_size):
        pl.semaphore_signal(
            barrier, inc=1, device_id={"ctx": lax.rem(me + step, ctx_size)}, device_id_type=MESH
        )
    for present, neighbour in ((place > 0, place - 1), (place < chan_size - 1, place + 1)):

        @pl.when(present)
        def _():
            pl.semaphore_signal(
                barrier, inc=1, device_id={"chan": neighbour}, device_id_type=MESH
            )

    sides = jnp.where(place > 0, 1, 0) + jnp.where(place < chan_size - 1, 1, 0)
    pl.semaphore_wait(barrier, ctx_size - 1 + sides)

    for part in range(len(parts)):

        @pl.when(place < chan_size - 1)
        def _():
            shard_copy(place, part, True, True).start()

        @pl.when(place > 0)
        def _():
            shard_copy(place, part, False, True).start()

    lanes = channels // SUB
    across = lanes // LANES

    def cut(index):
        return pl.ds(pl.multiple_of(index * LANES, LANES), LANES)

    def tiled(index, first, rows):
        return (lax.rem(index, across), pl.ds(first * SUB + index // across, rows, stride=SUB))

    def each_cut(action):
        for index in range(channels // LANES):
            action(index, slice(index * LANES, (index + 1) * LANES))

    def to_tiles(target, table):
        def action(index, cols):
            target[index % across, pl.ds(index // across, order, stride=SUB), :] = table[:, cols]

        each_cut(action)

    def from_tiles(source):
        return jnp.concatenate(
            [
                source[index % across, pl.ds(index // across, order, stride=SUB), :]
                for index in range(channels // LANES)
            ],
            axis=1,
        )

    def share_out(target, table):
        for other in range(ctx_size):
            target(other, table[:, other * width : (other + 1) * width])

    rate = decay_rates[...]
    to_tiles(decay, jnp.exp(-rate))
    to_tiles(gain, residues[...] * jnp.sqrt(2.0 * rate))

    @pl.loop(0, channels // LANES)
    def _(index):
        cols = cut(index)
        pair = keys[cols, :].astype(F32) * values[cols, :].astype(F32)
        v, rows = tiled(index, 0, tokens)
        source[v, rows, :] = rounded(pair).T
        gate[:, cols] = queries[cols, :].astype(F32).T

    def mode_rows(n):
        return slice(n * SUB, (n + 1) * SUB)

    def at(token):
        return pl.ds(pl.multiple_of(token * SUB, SUB), SUB)

    def load_modes(table, v, modes):
        return [table[v, mode_rows(n), :] for n in modes]

    def store_modes(table, v, modes, state):
        for n, value in zip(modes, state):
            table[v, mode_rows(n), :] = value

    every = range(order)
    zeros = tuple(jnp.zeros((SUB, LANES), F32) for _ in every)

    @pl.loop(0, across)
    def _(v):
        factors = load_modes(decay, v, every)

        def block(index, state):
            helds, moments = map(list, state)
            for step in range(STEP):
                row = source[v, at(index * STEP + step), :]
                for n in every:
                    moments[n] = factors[n] * (moments[n] + helds[n])
                    helds[n] = factors[n] * helds[n] + row
            return tuple(helds), tuple(moments)

        state = (zeros, zeros)
        steps = half // STEP
        for h in range(HALVES):
            if h:
                for kind in range(2):
                    store_modes(starts.at[h, kind], v, every, state[kind])
            state = lax.fori_loop(h * steps, (h + 1) * steps, block, state)
        store_modes(plain_sum, v, every, state[0])
        store_modes(moment_sum, v, every, state[1])

    def put(kind):
        def action(other, value):
            causal_end_out[other, kind] = value

        return action

    share_out(put(0), from_tiles(plain_sum))
    share_out(put(1), from_tiles(moment_sum))
    send_all(causal_end_links)

    for table in (plain_sum, moment_sum, held_now):
        table[...] = jnp.zeros(table.shape, F32)

    def multiply(lefts, shard, rows, first=False):
        @pl.loop(0, channels // tile)
        def _(index):
            cols = pl.ds(pl.multiple_of(index * tile, tile), tile)
            term = tree_sum(
                [
                    lax.dot_general(
                        left[...],
                        weight[shard, cols, taken],
                        (((1,), (1,)), ((), ())),
                        preferred_element_type=F32,
                    )
                    for left, taken in lefts
                ]
            )
            mixer[rows, cols] = term if first else mixer[rows, cols] + term

    everything = slice(None)
    weight_copy(place).wait()
    multiply([(out_grad, everything)], place, everything, True)

    def around(distance):
        return (
            (place - distance, place >= distance, place < chan_size - 1, True),
            (place + distance, place + distance < chan_size, place > 0, False),
        )

    def relay(distance):
        for part in range(len(parts)):
            for shard, present, onward, going_up in around(distance):

                @pl.when(present)
                def _():
                    shard_copy(shard, part, going_up).wait_recv()

                    @pl.when(onward)
                    def _():
                        shard_copy(shard, part, going_up).start()

    def take_whole(distance):
        for shard, present, onward, going_up in around(distance):

            @pl.when(present)
            def _():
                weight_copy(shard).wait()
                multiply(
                    [
                        (gathered.at[shard, e], pl.ds(e * piece, piece))
                        for e in range(SPLITS)
                    ],
                    shard,
                    everything,
                )

    own_rate = own_rates[:, own]
    own_far = jnp.exp(-own_rate * tokens)

    def causal_states():
        held = jnp.zeros((order, width), F32)
        moment = jnp.zeros((order, width), F32)
        for block in range(ctx_size):
            causal_in_out[block, 0] = held
            causal_in_out[block, 1] = moment
            if block < ctx_size - 1:
                await_slot(causal_end_links, block)
                moment = causal_end_in[block, 1] + own_far * (moment + float(tokens) * held)
                held = causal_end_in[block, 0] + own_far * held
        await_slot(causal_end_links, ctx_size - 1)
        send_all(causal_in_links)

    def causal_scan():
        for other in range(ctx_size):
            await_slot(causal_in_links, other)
            for kind in range(2):
                incoming[kind, :, other * width : (other + 1) * width] = causal_in_in[other, kind]
        for kind in range(2):
            to_tiles(starts.at[0, kind], incoming[kind])
        for h in range(1, HALVES):
            far = jnp.exp(-rate * float(h * half))
            plain = far * incoming[0]
            moment = far * (incoming[1] + float(h * half) * incoming[0])

            def action(index, cols):
                v, rows = index % across, pl.ds(index // across, order, stride=SUB)
                starts[h, 0, v, rows, :] = starts[h, 0, v, rows, :] + plain[:, cols]
                starts[h, 1, v, rows, :] = starts[h, 1, v, rows, :] + moment[:, cols]

            each_cut(action)

        @pl.loop(0, across)
        def _(v):
            factors = load_modes(decay, v, every)
            gains = load_modes(gain, v, every)

            def block(index, state):
                helds = list(state)
                for step in range(STEP):
                    where = (v, at(index * STEP + step))
                    row = source[where]
                    for n in every:
                        helds[n] = factors[n] * helds[n] + row
                    total = tree_sum([gains[n] * helds[n] for n in every])
                    conv[where] = rounded(total)
                return tuple(helds)

            lax.fori_loop(0, tokens // STEP, block, tuple(load_modes(starts.at[0, 0], v, every)))

    def drive_rows(h):
        @pl.loop(0, channels // LANES)
        def _(index):
            cols = cut(index)
            where = (pl.ds(h * half, half), cols)
            v, rows = tiled(index, h * half, half)
            drive[v, rows, :] = rounded(rounded(mixer[where]) * gate[where])

    def adjoint_scan(h):
        @pl.loop(0, across)
        def _(v):
            factors = load_modes(decay, v, every)
            gains = load_modes(gain, v, every)

            def block(index, state):
                helds = list(state)
                for step in range(STEP):
                    where = (v, at((h + 1) * half - 1 - index * STEP - step))
                    row = drive[where]
                    for n in every:
                        helds[n] = factors[n] * helds[n] + row
                    adjoint[where] = tree_sum([gains[n] * helds[n] for n in every])
                return tuple(helds)

            state = lax.fori_loop(0, half // STEP, block, tuple(load_modes(held_now, v, every)))
            store_modes(held_now, v, every, state)

    def sum_scan(h):
        @pl.loop(0, across)
        def _(v):
            for first in range(0, order, 8):
                modes = range(first, min(first + 8, order))
                factors = load_modes(decay, v, modes)

                def block(index, state):
                    helds, moments, plains, slopes = map(list, state)
                    for step in range(STEP):
                        where = (v, at(h * half + index * STEP + step))
                        row, push = source[where], drive[where]
                        for n in range(len(modes)):
                            moments[n] = factors[n] * (moments[n] + helds[n])
                            helds[n] = factors[n] * helds[n] + row
                            plains[n] = plains[n] + push * helds[n]
                            slopes[n] = slopes[n] + push * moments[n]
                    return tuple(map(tuple, (helds, moments, plains, slopes)))

                tables = (starts.at[h, 0], starts.at[h, 1], plain_sum, moment_sum)
                state = tuple(tuple(load_modes(table, v, modes)) for table in tables)
                state = lax.fori_loop(0, half // STEP, block, state)
                store_modes(plain_sum, v, modes, state[2])
                store_modes(moment_sum, v, modes, state[3])

    if chan_size > 2:
        relay(1)
    causal_states()
    if chan_size > 2:
        take_whole(1)
    causal_scan()
    for distance in range(2, chan_size - 1):
        relay(distance)
        take_whole(distance)

    last = jnp.where(place == 0, chan_size - 1, 0)
    at_end = (place == 0) | (place == chan_size - 1)

    if chan_size > 1:

        @pl.when(at_end)
        def _():
            weight_copy(last).wait()

    for h in reversed(range(HALVES)):
        if chan_size > 1:
            for part, (number, e) in enumerate(parts):
                if number == h:

                    @pl.when(at_end)
                    def _():
                        rows = pl.ds(h * half, half)
                        shard_copy(last, part, True).wait_recv()
                        multiply(
                            [(gathered.at[last, e, rows], pl.ds(e * piece, piece))], last, rows
                        )

        drive_rows(h)
        adjoint_scan(h)
        if h:
            sum_scan(h)

    def put_end(other, value):
        end_out[other] = value

    share_out(put_end, from_tiles(held_now))
    send_all(end_links)
    sum_scan(0)

    def put_sum(kind):
        def action(other, value):
            sums_out[other, kind] = value

        return action

    share_out(put_sum(0), from_tiles(plain_sum))
    share_out(put_sum(1), from_tiles(moment_sum))

    held = jnp.zeros((order, width), F32)
    for block in reversed(range(ctx_size)):
        start_out[block] = held
        send_or_keep(start_links, block)
        await_slot(end_links, block)
        if block:
            held = end_in[block] + own_far * held
    send_all(sums_links)

    @pl.loop(0, channels // LANES)
    def _(index):
        cols = cut(index)
        v, rows = tiled(index, 0, tokens)
        query_grad[cols, :] = (rounded(mixer[:, cols]) * conv[v, rows, :]).T.astype(BF16)

    for other in range(ctx_size):
        await_slot(start_links, other)
        incoming[0, :, other * width : (other + 1) * width] = start_in[other]
    to_tiles(held_now, incoming[0])

    @pl.loop(0, across)
    def _(v):
        factors = load_modes(decay, v, every)
        terms = [
            start * factor * scale
            for start, factor, scale in zip(
                load_modes(held_now, v, every), factors, load_modes(gain, v, every)
            )
        ]

        def block(index, state):
            state = list(state)
            for step in range(STEP):
                where = (v, at(tokens - 1 - index * STEP - step))
                adjoint[where] = adjoint[where] + tree_sum(list(state))
                state = [term * factor for term, factor in zip(state, factors)]
            return tuple(state)

        lax.fori_loop(0, tokens // STEP, block, tuple(terms))

    @pl.loop(0, channels // LANES)
    def _(index):
        cols = cut(index)
        v, rows = tiled(index, 0, tokens)
        result = rounded(adjoint[v, rows, :]).T
        key_grad[cols, :] = (result * values[cols, :].astype(F32)).astype(BF16)
        value_grad[cols, :] = (result * keys[cols, :].astype(F32)).astype(BF16)

    plain = jnp.zeros((order, width), F32)
    slope = jnp.zeros((order, width), F32)
    for other in range(ctx_size):
        await_slot(sums_links, other)
        plain = plain + sums_in[other, 0]
        slope = slope + sums_in[other, 1]
    root = jnp.sqrt(2.0 * own_rate)
    resid_grad[...] = root * plain
    decay_grad[...] = own_residues[:, own] * root * (0.5 * plain - own_rate * slope)

    @pl.loop(0, ctx_size)
    def _(other):
        @pl.when(other != me)
        def _():
            for link in (causal_end_links, causal_in_links, end_links, start_links, sums_links):
                exchange(link, other).wait_send()

    for distance in range(chan_size - 1):
        for shard, present, onward, going_up in around(distance):

            @pl.when(present & onward)
            def _():
                for part in range(len(parts)):
                    shard_copy(shard, part, going_up, distance == 0).wait_send()


def hand_over(*refs):
    number = len(refs) // 2
    copies = [
        pltpu.make_async_copy(refs[i], refs[number + i], refs[-1].at[i]) for i in range(number)
    ]
    for copy in copies:
        copy.start()
    for copy in copies:
        copy.wait()


def local(queries, keys, values, out_grad, out_weight, residues, decay_rates):
    channels, tokens = queries.shape
    chan_size = lax.axis_size("chan")
    ctx_size = lax.axis_size("ctx")
    width = channels // ctx_size
    depth = out_grad.shape[1]
    order = residues.shape[0]
    owned = residues, decay_rates
    if width % LANES:
        offset = lax.axis_index("ctx") * width
        owned = [lax.dynamic_slice_in_dim(x, offset, width, 1) for x in owned]
    number = HALVES * SPLITS
    gate = jax.ShapeDtypeStruct((channels, tokens), BF16)
    grads = jax.ShapeDtypeStruct((order, width), F32)
    shapes = (gate,) * 3 + (grads,) * 2
    vmem = pl.BlockSpec(memory_space=pltpu.VMEM)
    anywhere = pl.BlockSpec(memory_space=pl.ANY)
    dma = pltpu.SemaphoreType.DMA
    across = channels // SUB // LANES
    plane = pltpu.VMEM((tokens, channels), F32)
    tiles = pltpu.VMEM((across, tokens * SUB, LANES), F32)
    table = pltpu.VMEM((across, order * SUB, LANES), F32)
    single = pltpu.VMEM((ctx_size, order, width), F32)
    twice = pltpu.VMEM((ctx_size, 2, order, width), F32)
    results = pl.pallas_call(
        functools.partial(body, chan_size, ctx_size),
        out_shape=shapes,
        in_specs=[vmem, vmem, vmem, vmem, anywhere, vmem, vmem, vmem, vmem],
        out_specs=(vmem,) * 5,
        scratch_shapes=[
            pltpu.VMEM((chan_size, channels, depth), BF16),
            pltpu.VMEM((chan_size, SPLITS, tokens, depth // SPLITS), BF16),
            *[plane] * 2,
            *[tiles] * 4,
            *[table] * 5,
            pltpu.VMEM((HALVES, 2, across, order * SUB, LANES), F32),
            pltpu.VMEM((2, order, channels), F32),
            *[twice] * 4,
            *[single] * 4,
            *[twice] * 2,
            dma((chan_size,)),
            dma((chan_size, number)),
            dma((chan_size, number)),
            dma((chan_size, number)),
            dma((5, ctx_size)),
            dma((5, ctx_size)),
        ],
        compiler_params=pltpu.CompilerParams(
            collective_id=0, has_side_effects=True, vmem_limit_bytes=52 * 1024 * 1024
        ),
    )(queries, keys, values, out_grad, out_weight, residues, decay_rates, *owned)
    return pl.pallas_call(
        hand_over,
        out_shape=shapes,
        in_specs=[anywhere] * 5,
        out_specs=(anywhere,) * 5,
        scratch_shapes=[dma((5,))],
        compiler_params=pltpu.CompilerParams(vmem_limit_bytes=2 * 1024 * 1024),
    )(*results)


def solution(mesh):
    placed = (
        P("chan", "ctx"),
        P("chan", "ctx"),
        P("chan", "ctx"),
        P("ctx", "chan"),
        P("chan", None),
        P(None, "chan"),
        P(None, "chan"),
    )
    return jax.shard_map(
        local,
        mesh=mesh,
        in_specs=placed,
        out_specs=(
            P("chan", "ctx"),
            P("chan", "ctx"),
            P("chan", "ctx"),
            P(None, ("chan", "ctx")),
            P(None, ("chan", "ctx")),
        ),
        check_vma=False,
    )
```

```python
import jax
import jax.numpy as jnp
from jax import lax
from jax.experimental import pallas as pl
from jax.experimental.pallas import tpu as pltpu
from jax.sharding import PartitionSpec as P

STEP = 8
SUB = 8
LANES = 128
HALVES = 2
SPLITS = 2
MESH = pl.DeviceIdType.MESH
F32, BF16 = jnp.float32, jnp.bfloat16


def rounded(x):
    return x.astype(BF16).astype(F32)


def tree_sum(terms):
    while len(terms) > 1:
        terms = [a + b for a, b in zip(terms[::2], terms[1::2])] + (
            [terms[-1]] if len(terms) % 2 else []
        )
    return terms[0]


def body(
    chan_size,
    ctx_size,
    fetched,
    out_grad,
    out_weight,
    owned,
    query_grad,
    key_grad,
    value_grad,
    resid_grad,
    decay_grad,
    queries,
    keys,
    values,
    residues,
    decay_rates,
    weight,
    gathered,
    gate,
    mixer,
    source,
    drive,
    conv,
    adjoint,
    decay,
    gain,
    held_now,
    plain_sum,
    moment_sum,
    starts,
    incoming,
    causal_end_out,
    causal_end_in,
    causal_in_out,
    causal_in_in,
    end_out,
    end_in,
    start_out,
    start_in,
    sums_out,
    sums_in,
    fetch_sems,
    weight_sems,
    shard_arrivals,
    up_sends,
    down_sends,
    sends,
    arrivals,
):
    place = lax.axis_index("chan")
    me = lax.axis_index("ctx")
    channels, tokens = queries.shape
    depth = out_grad.shape[1]
    width = channels // ctx_size
    order = residues.shape[0]
    count = order // 8
    half = tokens // HALVES
    piece = depth // SPLITS
    own = slice(None)
    if not owned:
        own = pl.ds(pl.multiple_of(me * width, width), width)
    own_residues, own_rates = owned or (residues, decay_rates)
    tile = channels

    def links(kind, outgoing, incoming):
        return (outgoing, incoming, sends.at[kind], arrivals.at[kind])

    causal_end_links = links(0, causal_end_out, causal_end_in)
    causal_in_links = links(1, causal_in_out, causal_in_in)
    end_links = links(2, end_out, end_in)
    start_links = links(3, start_out, start_in)
    sums_links = links(4, sums_out, sums_in)

    def exchange(link, other):
        outgoing, incoming, sent, arrived = link
        return pltpu.make_async_remote_copy(
            src_ref=outgoing.at[other],
            dst_ref=incoming.at[me],
            send_sem=sent.at[other],
            recv_sem=arrived.at[me],
            device_id={"ctx": other},
            device_id_type=MESH,
        )

    def send_or_keep(link, other):
        @pl.when(other != me)
        def _():
            exchange(link, other).start()

        @pl.when(other == me)
        def _():
            link[1][me] = link[0][me]

    def await_slot(link, other):
        outgoing, incoming, sent, arrived = link

        @pl.when(other != me)
        def _():
            pltpu.make_async_remote_copy(
                src_ref=outgoing.at[other],
                dst_ref=incoming.at[other],
                send_sem=sent.at[other],
                recv_sem=arrived.at[other],
                device_id={"ctx": other},
                device_id_type=MESH,
            ).wait_recv()

    def send_all(link):
        @pl.loop(0, ctx_size)
        def _(step):
            send_or_keep(link, lax.rem(me + 1 + step, ctx_size))

    def weight_copy(shard):
        return pltpu.make_async_copy(
            out_weight.at[:, pl.ds(pl.multiple_of(shard * depth, depth), depth)],
            weight.at[shard],
            weight_sems.at[shard],
        )

    parts = [(h, e) for h in reversed(range(HALVES)) for e in range(SPLITS)]

    def shard_copy(shard, part, going_up, first=False):
        h, e = parts[part]
        rows, cols = pl.ds(h * half, half), pl.ds(e * piece, piece)
        return pltpu.make_async_remote_copy(
            src_ref=out_grad.at[rows, cols] if first else gathered.at[shard, e, rows],
            dst_ref=gathered.at[shard, e, rows],
            send_sem=(up_sends if going_up else down_sends).at[shard, part],
            recv_sem=shard_arrivals.at[shard, part],
            device_id={"chan": place + 1 if going_up else place - 1},
            device_id_type=MESH,
        )

    fetches = [
        pltpu.make_async_copy(remote, near, fetch_sems.at[i])
        for i, (remote, near) in enumerate(
            zip(fetched, (queries, keys, values, residues, decay_rates))
        )
    ] + [
        pltpu.make_async_copy(
            out_grad.at[:, pl.ds(e * piece, piece)], gathered.at[place, e], fetch_sems.at[5 + e]
        )
        for e in range(SPLITS)
    ]

    barrier = pltpu.get_barrier_semaphore()
    for step in range(1, ctx_size):
        pl.semaphore_signal(
            barrier, inc=1, device_id={"ctx": lax.rem(me + step, ctx_size)}, device_id_type=MESH
        )
    for present, neighbour in ((place > 0, place - 1), (place < chan_size - 1, place + 1)):

        @pl.when(present)
        def _():
            pl.semaphore_signal(
                barrier, inc=1, device_id={"chan": neighbour}, device_id_type=MESH
            )

    sides = jnp.where(place > 0, 1, 0) + jnp.where(place < chan_size - 1, 1, 0)
    pl.semaphore_wait(barrier, ctx_size - 1 + sides)

    for part in range(len(parts)):

        @pl.when(place < chan_size - 1)
        def _():
            shard_copy(place, part, True, True).start()

        @pl.when(place > 0)
        def _():
            shard_copy(place, part, False, True).start()

    for fetch in fetches:
        fetch.start()
    weight_copy(place).start()
    for distance in range(1, chan_size):
        for shard, present in (
            (place - distance, place >= distance),
            (place + distance, place + distance < chan_size),
        ):

            @pl.when(present)
            def _():
                weight_copy(shard).start()
    for fetch in fetches:
        fetch.wait()

    lanes = channels // SUB
    across = lanes // LANES

    def cut(index):
        return pl.ds(pl.multiple_of(index * LANES, LANES), LANES)

    def tiled(index, first, rows):
        return (lax.rem(index, across), pl.ds(first * SUB + index // across, rows, stride=SUB))

    def each_cut(action):
        for index in range(channels // LANES):
            action(index, slice(index * LANES, (index + 1) * LANES))

    def to_tiles(target, table):
        def action(index, cols):
            target[index % across, pl.ds(index // across, order, stride=SUB), :] = table[:, cols]

        each_cut(action)

    def from_tiles(source):
        return jnp.concatenate(
            [
                source[index % across, pl.ds(index // across, order, stride=SUB), :]
                for index in range(channels // LANES)
            ],
            axis=1,
        )

    def share_out(target, table):
        for other in range(ctx_size):
            target(other, table[:, other * width : (other + 1) * width])

    rate = decay_rates[...]
    to_tiles(decay, jnp.exp(-rate))
    to_tiles(gain, residues[...] * jnp.sqrt(2.0 * rate))

    @pl.loop(0, channels // LANES)
    def _(index):
        cols = cut(index)
        pair = keys[cols, :].astype(F32) * values[cols, :].astype(F32)
        v, rows = tiled(index, 0, tokens)
        source[v, rows, :] = rounded(pair).T
        gate[:, cols] = queries[cols, :].astype(F32).T

    def mode_rows(n):
        return slice(n * SUB, (n + 1) * SUB)

    def at(token):
        return pl.ds(pl.multiple_of(token * SUB, SUB), SUB)

    def load_modes(table, v, modes):
        return [table[v, mode_rows(n), :] for n in modes]

    def store_modes(table, v, modes, state):
        for n, value in zip(modes, state):
            table[v, mode_rows(n), :] = value

    every = range(order)
    zeros = tuple(jnp.zeros((SUB, LANES), F32) for _ in every)

    @pl.loop(0, across)
    def _(v):
        factors = load_modes(decay, v, every)

        def block(index, state):
            helds, moments = map(list, state)
            for step in range(STEP):
                row = source[v, at(index * STEP + step), :]
                for n in every:
                    moments[n] = factors[n] * (moments[n] + helds[n])
                    helds[n] = factors[n] * helds[n] + row
            return tuple(helds), tuple(moments)

        state = (zeros, zeros)
        steps = half // STEP
        for h in range(HALVES):
            if h:
                for kind in range(2):
                    store_modes(starts.at[h, kind], v, every, state[kind])
            state = lax.fori_loop(h * steps, (h + 1) * steps, block, state)
        store_modes(plain_sum, v, every, state[0])
        store_modes(moment_sum, v, every, state[1])

    def put(kind):
        def action(other, value):
            causal_end_out[other, kind] = value

        return action

    share_out(put(0), from_tiles(plain_sum))
    share_out(put(1), from_tiles(moment_sum))
    send_all(causal_end_links)

    for table in (plain_sum, moment_sum, held_now):
        table[...] = jnp.zeros(table.shape, F32)

    def multiply(lefts, shard, rows, first=False):
        @pl.loop(0, channels // tile)
        def _(index):
            cols = pl.ds(pl.multiple_of(index * tile, tile), tile)
            term = tree_sum(
                [
                    lax.dot_general(
                        left[...],
                        weight[shard, cols, taken],
                        (((1,), (1,)), ((), ())),
                        preferred_element_type=F32,
                    )
                    for left, taken in lefts
                ]
            )
            mixer[rows, cols] = term if first else mixer[rows, cols] + term

    everything = slice(None)
    weight_copy(place).wait()
    multiply(
        [(gathered.at[place, e], pl.ds(e * piece, piece)) for e in range(SPLITS)],
        place,
        everything,
        True,
    )

    def around(distance):
        return (
            (place - distance, place >= distance, place < chan_size - 1, True),
            (place + distance, place + distance < chan_size, place > 0, False),
        )

    def relay(distance):
        for part in range(len(parts)):
            for shard, present, onward, going_up in around(distance):

                @pl.when(present)
                def _():
                    shard_copy(shard, part, going_up).wait_recv()

                    @pl.when(onward)
                    def _():
                        shard_copy(shard, part, going_up).start()

    def take_whole(distance):
        for shard, present, onward, going_up in around(distance):

            @pl.when(present)
            def _():
                weight_copy(shard).wait()
                multiply(
                    [
                        (gathered.at[shard, e], pl.ds(e * piece, piece))
                        for e in range(SPLITS)
                    ],
                    shard,
                    everything,
                )

    own_rate = own_rates[:, own]
    own_far = jnp.exp(-own_rate * tokens)

    def causal_states():
        held = jnp.zeros((order, width), F32)
        moment = jnp.zeros((order, width), F32)
        for block in range(ctx_size):
            causal_in_out[block, 0] = held
            causal_in_out[block, 1] = moment
            if block < ctx_size - 1:
                await_slot(causal_end_links, block)
                moment = causal_end_in[block, 1] + own_far * (moment + float(tokens) * held)
                held = causal_end_in[block, 0] + own_far * held
        await_slot(causal_end_links, ctx_size - 1)
        send_all(causal_in_links)

    def causal_scan():
        for other in range(ctx_size):
            await_slot(causal_in_links, other)
            for kind in range(2):
                incoming[kind, :, other * width : (other + 1) * width] = causal_in_in[other, kind]
        for kind in range(2):
            to_tiles(starts.at[0, kind], incoming[kind])
        for h in range(1, HALVES):
            far = jnp.exp(-rate * float(h * half))
            plain = far * incoming[0]
            moment = far * (incoming[1] + float(h * half) * incoming[0])

            def action(index, cols):
                v, rows = index % across, pl.ds(index // across, order, stride=SUB)
                starts[h, 0, v, rows, :] = starts[h, 0, v, rows, :] + plain[:, cols]
                starts[h, 1, v, rows, :] = starts[h, 1, v, rows, :] + moment[:, cols]

            each_cut(action)

        @pl.loop(0, across)
        def _(v):
            factors = load_modes(decay, v, every)
            gains = load_modes(gain, v, every)

            def block(index, state):
                helds = list(state)
                for step in range(STEP):
                    where = (v, at(index * STEP + step))
                    row = source[where]
                    for n in every:
                        helds[n] = factors[n] * helds[n] + row
                    total = tree_sum([gains[n] * helds[n] for n in every])
                    conv[where] = rounded(total)
                return tuple(helds)

            lax.fori_loop(0, tokens // STEP, block, tuple(load_modes(starts.at[0, 0], v, every)))

    def drive_rows(h):
        @pl.loop(0, channels // LANES)
        def _(index):
            cols = cut(index)
            where = (pl.ds(h * half, half), cols)
            v, rows = tiled(index, h * half, half)
            drive[v, rows, :] = rounded(rounded(mixer[where]) * gate[where])

    def adjoint_scan(h):
        @pl.loop(0, across)
        def _(v):
            factors = load_modes(decay, v, every)
            gains = load_modes(gain, v, every)

            def block(index, state):
                helds = list(state)
                for step in range(STEP):
                    where = (v, at((h + 1) * half - 1 - index * STEP - step))
                    row = drive[where]
                    for n in every:
                        helds[n] = factors[n] * helds[n] + row
                    adjoint[where] = tree_sum([gains[n] * helds[n] for n in every])
                return tuple(helds)

            state = lax.fori_loop(0, half // STEP, block, tuple(load_modes(held_now, v, every)))
            store_modes(held_now, v, every, state)

    def sum_scan(h):
        @pl.loop(0, across)
        def _(v):
            for first in range(0, order, 8):
                modes = range(first, min(first + 8, order))
                factors = load_modes(decay, v, modes)

                def block(index, state):
                    helds, moments, plains, slopes = map(list, state)
                    for step in range(STEP):
                        where = (v, at(h * half + index * STEP + step))
                        row, push = source[where], drive[where]
                        for n in range(len(modes)):
                            moments[n] = factors[n] * (moments[n] + helds[n])
                            helds[n] = factors[n] * helds[n] + row
                            plains[n] = plains[n] + push * helds[n]
                            slopes[n] = slopes[n] + push * moments[n]
                    return tuple(map(tuple, (helds, moments, plains, slopes)))

                tables = (starts.at[h, 0], starts.at[h, 1], plain_sum, moment_sum)
                state = tuple(tuple(load_modes(table, v, modes)) for table in tables)
                state = lax.fori_loop(0, half // STEP, block, state)
                store_modes(plain_sum, v, modes, state[2])
                store_modes(moment_sum, v, modes, state[3])

    if chan_size > 2:
        relay(1)
    causal_states()
    if chan_size > 2:
        take_whole(1)
    causal_scan()
    for distance in range(2, chan_size - 1):
        relay(distance)
        take_whole(distance)

    last = jnp.where(place == 0, chan_size - 1, 0)
    at_end = (place == 0) | (place == chan_size - 1)

    if chan_size > 1:

        @pl.when(at_end)
        def _():
            weight_copy(last).wait()

    for h in reversed(range(HALVES)):
        if chan_size > 1:
            for part, (number, e) in enumerate(parts):
                if number == h:

                    @pl.when(at_end)
                    def _():
                        rows = pl.ds(h * half, half)
                        shard_copy(last, part, True).wait_recv()
                        multiply(
                            [(gathered.at[last, e, rows], pl.ds(e * piece, piece))], last, rows
                        )

        drive_rows(h)
        adjoint_scan(h)

    def put_end(other, value):
        end_out[other] = value

    share_out(put_end, from_tiles(held_now))
    send_all(end_links)
    sum_scan(HALVES - 1)

    held = jnp.zeros((order, width), F32)
    for block in reversed(range(ctx_size)):
        start_out[block] = held
        send_or_keep(start_links, block)
        await_slot(end_links, block)
        if block:
            held = end_in[block] + own_far * held
    for h in range(HALVES - 1):
        sum_scan(h)

    def put_sum(kind):
        def action(other, value):
            sums_out[other, kind] = value

        return action

    share_out(put_sum(0), from_tiles(plain_sum))
    share_out(put_sum(1), from_tiles(moment_sum))

    send_all(sums_links)

    for other in range(ctx_size):
        await_slot(start_links, other)
        incoming[0, :, other * width : (other + 1) * width] = start_in[other]
    to_tiles(held_now, incoming[0])

    @pl.loop(0, across)
    def _(v):
        factors = load_modes(decay, v, every)
        terms = [
            start * factor * scale
            for start, factor, scale in zip(
                load_modes(held_now, v, every), factors, load_modes(gain, v, every)
            )
        ]

        def block(index, state):
            state = list(state)
            for step in range(STEP):
                where = (v, at(tokens - 1 - index * STEP - step))
                adjoint[where] = adjoint[where] + tree_sum(list(state))
                state = [term * factor for term, factor in zip(state, factors)]
            return tuple(state)

        lax.fori_loop(0, tokens // STEP, block, tuple(terms))

    @pl.loop(0, channels // LANES)
    def _(index):
        cols = cut(index)
        v, rows = tiled(index, 0, tokens)
        result = rounded(adjoint[v, rows, :]).T
        key_grad[cols, :] = (result * values[cols, :].astype(F32)).astype(BF16)
        value_grad[cols, :] = (result * keys[cols, :].astype(F32)).astype(BF16)

    @pl.loop(0, channels // LANES)
    def _(index):
        cols = cut(index)
        v, rows = tiled(index, 0, tokens)
        query_grad[cols, :] = (rounded(mixer[:, cols]) * conv[v, rows, :]).T.astype(BF16)

    plain = jnp.zeros((order, width), F32)
    slope = jnp.zeros((order, width), F32)
    for other in range(ctx_size):
        await_slot(sums_links, other)
        plain = plain + sums_in[other, 0]
        slope = slope + sums_in[other, 1]
    root = jnp.sqrt(2.0 * own_rate)
    resid_grad[...] = root * plain
    decay_grad[...] = own_residues[:, own] * root * (0.5 * plain - own_rate * slope)

    @pl.loop(0, ctx_size)
    def _(other):
        @pl.when(other != me)
        def _():
            for link in (causal_end_links, causal_in_links, end_links, start_links, sums_links):
                exchange(link, other).wait_send()

    for distance in range(chan_size - 1):
        for shard, present, onward, going_up in around(distance):

            @pl.when(present & onward)
            def _():
                for part in range(len(parts)):
                    shard_copy(shard, part, going_up, distance == 0).wait_send()


def hand_over(*refs):
    number = len(refs) // 2
    copies = [
        pltpu.make_async_copy(refs[i], refs[number + i], refs[-1].at[i]) for i in range(number)
    ]
    for copy in copies:
        copy.start()
    for copy in copies:
        copy.wait()


def local(queries, keys, values, out_grad, out_weight, residues, decay_rates):
    channels, tokens = queries.shape
    chan_size = lax.axis_size("chan")
    ctx_size = lax.axis_size("ctx")
    width = channels // ctx_size
    depth = out_grad.shape[1]
    order = residues.shape[0]
    owned = []
    if width % LANES:
        offset = lax.axis_index("ctx") * width
        owned = [lax.dynamic_slice_in_dim(x, offset, width, 1) for x in (residues, decay_rates)]
    number = HALVES * SPLITS
    gate = jax.ShapeDtypeStruct((channels, tokens), BF16)
    grads = jax.ShapeDtypeStruct((order, width), F32)
    shapes = (gate,) * 3 + (grads,) * 2
    vmem = pl.BlockSpec(memory_space=pltpu.VMEM)
    anywhere = pl.BlockSpec(memory_space=pl.ANY)
    dma = pltpu.SemaphoreType.DMA
    across = channels // SUB // LANES
    plane = pltpu.VMEM((tokens, channels), F32)
    tiles = pltpu.VMEM((across, tokens * SUB, LANES), F32)
    table = pltpu.VMEM((across, order * SUB, LANES), F32)
    single = pltpu.VMEM((ctx_size, order, width), F32)
    twice = pltpu.VMEM((ctx_size, 2, order, width), F32)
    def call(*refs):
        taken = 7 + len(owned)
        body(chan_size, ctx_size, refs[:5], *refs[5:7], refs[7:taken], *refs[taken:])

    results = pl.pallas_call(
        call,
        out_shape=shapes,
        in_specs=[pl.BlockSpec(memory_space=pltpu.HBM)] * 7 + [vmem] * len(owned),
        out_specs=(vmem,) * 5,
        scratch_shapes=[
            *[pltpu.VMEM((channels, tokens), BF16)] * 3,
            *[pltpu.VMEM((order, channels), F32)] * 2,
            pltpu.VMEM((chan_size, channels, depth), BF16),
            pltpu.VMEM((chan_size, SPLITS, tokens, depth // SPLITS), BF16),
            *[plane] * 2,
            *[tiles] * 4,
            *[table] * 5,
            pltpu.VMEM((HALVES, 2, across, order * SUB, LANES), F32),
            pltpu.VMEM((2, order, channels), F32),
            *[twice] * 4,
            *[single] * 4,
            *[twice] * 2,
            dma((5 + SPLITS,)),
            dma((chan_size,)),
            dma((chan_size, number)),
            dma((chan_size, number)),
            dma((chan_size, number)),
            dma((5, ctx_size)),
            dma((5, ctx_size)),
        ],
        compiler_params=pltpu.CompilerParams(
            collective_id=0, has_side_effects=True, vmem_limit_bytes=52 * 1024 * 1024
        ),
    )(queries, keys, values, residues, decay_rates, out_grad, out_weight, *owned)
    return pl.pallas_call(
        hand_over,
        out_shape=shapes,
        in_specs=[anywhere] * 5,
        out_specs=(anywhere,) * 5,
        scratch_shapes=[dma((5,))],
        compiler_params=pltpu.CompilerParams(vmem_limit_bytes=2 * 1024 * 1024),
    )(*results)


def solution(mesh):
    placed = (
        P("chan", "ctx"),
        P("chan", "ctx"),
        P("chan", "ctx"),
        P("ctx", "chan"),
        P("chan", None),
        P(None, "chan"),
        P(None, "chan"),
    )
    return jax.shard_map(
        local,
        mesh=mesh,
        in_specs=placed,
        out_specs=(
            P("chan", "ctx"),
            P("chan", "ctx"),
            P("chan", "ctx"),
            P(None, ("chan", "ctx")),
            P(None, ("chan", "ctx")),
        ),
        check_vma=False,
    )
```

```python
import jax
import jax.numpy as jnp
from jax import lax
from jax.experimental import pallas as pl
from jax.experimental.pallas import tpu as pltpu
from jax.sharding import PartitionSpec as P

STEP = 8
SUB = 8
LANES = 128
HALVES = 2
SPLITS = 2
MESH = pl.DeviceIdType.MESH
F32, BF16 = jnp.float32, jnp.bfloat16


def rounded(x):
    return x.astype(BF16).astype(F32)


def tree_sum(terms):
    while len(terms) > 1:
        terms = [a + b for a, b in zip(terms[::2], terms[1::2])] + (
            [terms[-1]] if len(terms) % 2 else []
        )
    return terms[0]


def body(
    chan_size,
    ctx_size,
    fetched,
    out_grad,
    out_weight,
    owned,
    query_grad,
    key_grad,
    value_grad,
    resid_grad,
    decay_grad,
    queries,
    keys,
    values,
    residues,
    decay_rates,
    weight,
    gathered,
    gate,
    mixer,
    source,
    drive,
    conv,
    adjoint,
    decay,
    gain,
    held_now,
    plain_sum,
    moment_sum,
    starts,
    incoming,
    causal_end_out,
    causal_end_in,
    causal_in_out,
    causal_in_in,
    end_out,
    end_in,
    start_out,
    start_in,
    sums_out,
    sums_in,
    fetch_sems,
    weight_sems,
    shard_arrivals,
    up_sends,
    down_sends,
    sends,
    arrivals,
):
    place = lax.axis_index("chan")
    me = lax.axis_index("ctx")
    channels, tokens = queries.shape
    depth = out_grad.shape[1]
    width = channels // ctx_size
    order = residues.shape[0]
    count = order // 8
    half = tokens // HALVES
    piece = depth // SPLITS
    own = slice(None)
    if not owned:
        own = pl.ds(pl.multiple_of(me * width, width), width)
    own_rates = owned[0] if owned else decay_rates
    tile = channels

    def links(kind, outgoing, incoming):
        return (outgoing, incoming, sends.at[kind], arrivals.at[kind])

    causal_end_links = links(0, causal_end_out, causal_end_in)
    causal_in_links = links(1, causal_in_out, causal_in_in)
    end_links = links(2, end_out, end_in)
    start_links = links(3, start_out, start_in)
    sums_links = links(4, sums_out, sums_in)

    def exchange(link, other):
        outgoing, incoming, sent, arrived = link
        return pltpu.make_async_remote_copy(
            src_ref=outgoing.at[other],
            dst_ref=incoming.at[me],
            send_sem=sent.at[other],
            recv_sem=arrived.at[me],
            device_id={"ctx": other},
            device_id_type=MESH,
        )

    def send_or_keep(link, other):
        @pl.when(other != me)
        def _():
            exchange(link, other).start()

        @pl.when(other == me)
        def _():
            link[1][me] = link[0][me]

    def await_slot(link, other):
        outgoing, incoming, sent, arrived = link

        @pl.when(other != me)
        def _():
            pltpu.make_async_remote_copy(
                src_ref=outgoing.at[other],
                dst_ref=incoming.at[other],
                send_sem=sent.at[other],
                recv_sem=arrived.at[other],
                device_id={"ctx": other},
                device_id_type=MESH,
            ).wait_recv()

    def send_all(link):
        @pl.loop(0, ctx_size)
        def _(step):
            send_or_keep(link, lax.rem(me + 1 + step, ctx_size))

    def weight_copy(shard):
        return pltpu.make_async_copy(
            out_weight.at[:, pl.ds(pl.multiple_of(shard * depth, depth), depth)],
            weight.at[shard],
            weight_sems.at[shard],
        )

    parts = [(h, e) for h in reversed(range(HALVES)) for e in range(SPLITS)]

    def shard_copy(shard, part, going_up, first=False):
        h, e = parts[part]
        rows, cols = pl.ds(h * half, half), pl.ds(e * piece, piece)
        return pltpu.make_async_remote_copy(
            src_ref=out_grad.at[rows, cols] if first else gathered.at[shard, e, rows],
            dst_ref=gathered.at[shard, e, rows],
            send_sem=(up_sends if going_up else down_sends).at[shard, part],
            recv_sem=shard_arrivals.at[shard, part],
            device_id={"chan": place + 1 if going_up else place - 1},
            device_id_type=MESH,
        )

    fetches = [
        pltpu.make_async_copy(remote, near, fetch_sems.at[i])
        for i, (remote, near) in enumerate(
            zip(fetched, (queries, keys, values, residues, decay_rates))
        )
    ] + [
        pltpu.make_async_copy(
            out_grad.at[:, pl.ds(e * piece, piece)], gathered.at[place, e], fetch_sems.at[5 + e]
        )
        for e in range(SPLITS)
    ]

    for fetch in fetches:
        fetch.start()
    weight_copy(place).start()
    barrier = pltpu.get_barrier_semaphore()
    for step in range(1, ctx_size):
        pl.semaphore_signal(
            barrier, inc=1, device_id={"ctx": lax.rem(me + step, ctx_size)}, device_id_type=MESH
        )
    for present, neighbour in ((place > 0, place - 1), (place < chan_size - 1, place + 1)):

        @pl.when(present)
        def _():
            pl.semaphore_signal(
                barrier, inc=1, device_id={"chan": neighbour}, device_id_type=MESH
            )

    sides = jnp.where(place > 0, 1, 0) + jnp.where(place < chan_size - 1, 1, 0)
    pl.semaphore_wait(barrier, ctx_size - 1 + sides)

    for part in range(len(parts)):

        @pl.when(place < chan_size - 1)
        def _():
            shard_copy(place, part, True, True).start()

        @pl.when(place > 0)
        def _():
            shard_copy(place, part, False, True).start()

    for fetch in fetches:
        fetch.wait()
    for distance in range(1, chan_size):
        for shard, present in (
            (place - distance, place >= distance),
            (place + distance, place + distance < chan_size),
        ):

            @pl.when(present)
            def _():
                weight_copy(shard).start()

    lanes = channels // SUB
    across = lanes // LANES

    def cut(index):
        return pl.ds(pl.multiple_of(index * LANES, LANES), LANES)

    def tiled(index, first, rows):
        return (lax.rem(index, across), pl.ds(first * SUB + index // across, rows, stride=SUB))

    def each_cut(action):
        for index in range(channels // LANES):
            action(index, slice(index * LANES, (index + 1) * LANES))

    def to_tiles(target, table):
        def action(index, cols):
            target[index % across, pl.ds(index // across, order, stride=SUB), :] = table[:, cols]

        each_cut(action)

    def from_tiles(source):
        return jnp.concatenate(
            [
                source[index % across, pl.ds(index // across, order, stride=SUB), :]
                for index in range(channels // LANES)
            ],
            axis=1,
        )

    def share_out(target, table):
        for other in range(ctx_size):
            target(other, table[:, other * width : (other + 1) * width])

    rate = decay_rates[...]
    to_tiles(decay, jnp.exp(-rate))
    to_tiles(gain, residues[...] * jnp.sqrt(2.0 * rate))

    @pl.loop(0, channels // LANES)
    def _(index):
        cols = cut(index)
        pair = keys[cols, :].astype(F32) * values[cols, :].astype(F32)
        v, rows = tiled(index, 0, tokens)
        source[v, rows, :] = rounded(pair).T
        gate[:, cols] = queries[cols, :].astype(F32).T

    def mode_rows(n):
        return slice(n * SUB, (n + 1) * SUB)

    def at(token):
        return pl.ds(pl.multiple_of(token * SUB, SUB), SUB)

    def load_modes(table, v, modes):
        return [table[v, mode_rows(n), :] for n in modes]

    def store_modes(table, v, modes, state):
        for n, value in zip(modes, state):
            table[v, mode_rows(n), :] = value

    every = range(order)
    zeros = tuple(jnp.zeros((SUB, LANES), F32) for _ in every)

    @pl.loop(0, across)
    def _(v):
        factors = load_modes(decay, v, every)

        def block(index, state):
            helds, moments = map(list, state)
            for step in range(STEP):
                row = source[v, at(index * STEP + step), :]
                for n in every:
                    moments[n] = factors[n] * (moments[n] + helds[n])
                    helds[n] = factors[n] * helds[n] + row
            return tuple(helds), tuple(moments)

        state = (zeros, zeros)
        steps = half // STEP
        for h in range(HALVES):
            if h:
                for kind in range(2):
                    store_modes(starts.at[h, kind], v, every, state[kind])
            state = lax.fori_loop(h * steps, (h + 1) * steps, block, state)
        store_modes(plain_sum, v, every, state[0])
        store_modes(moment_sum, v, every, state[1])

    def put(kind):
        def action(other, value):
            causal_end_out[other, kind] = value

        return action

    share_out(put(0), from_tiles(plain_sum))
    share_out(put(1), from_tiles(moment_sum))
    send_all(causal_end_links)

    for table in (plain_sum, moment_sum, held_now):
        table[...] = jnp.zeros(table.shape, F32)

    def multiply(lefts, shard, rows, first=False):
        @pl.loop(0, channels // tile)
        def _(index):
            cols = pl.ds(pl.multiple_of(index * tile, tile), tile)
            term = tree_sum(
                [
                    lax.dot_general(
                        left[...],
                        weight[shard, cols, taken],
                        (((1,), (1,)), ((), ())),
                        preferred_element_type=F32,
                    )
                    for left, taken in lefts
                ]
            )
            mixer[rows, cols] = term if first else mixer[rows, cols] + term

    everything = slice(None)
    weight_copy(place).wait()
    multiply(
        [(gathered.at[place, e], pl.ds(e * piece, piece)) for e in range(SPLITS)],
        place,
        everything,
        True,
    )

    def around(distance):
        return (
            (place - distance, place >= distance, place < chan_size - 1, True),
            (place + distance, place + distance < chan_size, place > 0, False),
        )

    paced = chan_size - 2

    def relay(distance):
        for part in range(len(parts)):
            for shard, present, onward, going_up in around(distance):

                @pl.when(present)
                def _():
                    shard_copy(shard, part, going_up).wait_recv()

                    if distance != paced or part < 2:

                        @pl.when(onward)
                        def _():
                            shard_copy(shard, part, going_up).start()

    def pace(part):
        if paced < 1:
            return
        for shard, present, onward, going_up in around(paced):

            @pl.when(present & onward)
            def _():
                shard_copy(shard, part - 2, going_up).wait_send()
                shard_copy(shard, part, going_up).start()

    def take_whole(distance):
        for shard, present, onward, going_up in around(distance):

            @pl.when(present)
            def _():
                weight_copy(shard).wait()
                multiply(
                    [
                        (gathered.at[shard, e], pl.ds(e * piece, piece))
                        for e in range(SPLITS)
                    ],
                    shard,
                    everything,
                )

    own_rate = own_rates[:, own]
    own_far = jnp.exp(-own_rate * tokens)

    def causal_states():
        held = jnp.zeros((order, width), F32)
        moment = jnp.zeros((order, width), F32)
        for block in range(ctx_size):
            causal_in_out[block, 0] = held
            causal_in_out[block, 1] = moment
            if block < ctx_size - 1:
                await_slot(causal_end_links, block)
                moment = causal_end_in[block, 1] + own_far * (moment + float(tokens) * held)
                held = causal_end_in[block, 0] + own_far * held
        await_slot(causal_end_links, ctx_size - 1)
        send_all(causal_in_links)

    def causal_scan():
        for other in range(ctx_size):
            await_slot(causal_in_links, other)
            for kind in range(2):
                incoming[kind, :, other * width : (other + 1) * width] = causal_in_in[other, kind]
        for kind in range(2):
            to_tiles(starts.at[0, kind], incoming[kind])
        for h in range(1, HALVES):
            far = jnp.exp(-rate * float(h * half))
            plain = far * incoming[0]
            moment = far * (incoming[1] + float(h * half) * incoming[0])

            def action(index, cols):
                v, rows = index % across, pl.ds(index // across, order, stride=SUB)
                starts[h, 0, v, rows, :] = starts[h, 0, v, rows, :] + plain[:, cols]
                starts[h, 1, v, rows, :] = starts[h, 1, v, rows, :] + moment[:, cols]

            each_cut(action)

        @pl.loop(0, across)
        def _(v):
            factors = load_modes(decay, v, every)
            gains = load_modes(gain, v, every)

            def block(index, state):
                helds = list(state)
                for step in range(STEP):
                    where = (v, at(index * STEP + step))
                    row = source[where]
                    for n in every:
                        helds[n] = factors[n] * helds[n] + row
                    total = tree_sum([gains[n] * helds[n] for n in every])
                    conv[where] = rounded(total)
                return tuple(helds)

            lax.fori_loop(0, tokens // STEP, block, tuple(load_modes(starts.at[0, 0], v, every)))

    def drive_rows(h):
        @pl.loop(0, channels // LANES)
        def _(index):
            cols = cut(index)
            where = (pl.ds(h * half, half), cols)
            v, rows = tiled(index, h * half, half)
            drive[v, rows, :] = rounded(rounded(mixer[where]) * gate[where])

    def adjoint_scan(h):
        @pl.loop(0, across)
        def _(v):
            factors = load_modes(decay, v, every)
            gains = load_modes(gain, v, every)

            def block(index, state):
                helds = list(state)
                for step in range(STEP):
                    where = (v, at((h + 1) * half - 1 - index * STEP - step))
                    row = drive[where]
                    for n in every:
                        helds[n] = factors[n] * helds[n] + row
                    adjoint[where] = tree_sum([gains[n] * helds[n] for n in every])
                return tuple(helds)

            state = lax.fori_loop(0, half // STEP, block, tuple(load_modes(held_now, v, every)))
            store_modes(held_now, v, every, state)

    def sum_scan(h):
        @pl.loop(0, across)
        def _(v):
            for first in range(0, order, 8):
                modes = range(first, min(first + 8, order))
                factors = load_modes(decay, v, modes)

                def block(index, state):
                    helds, moments, plains, slopes = map(list, state)
                    for step in range(STEP):
                        where = (v, at(h * half + index * STEP + step))
                        row, push = source[where], drive[where]
                        for n in range(len(modes)):
                            moments[n] = factors[n] * (moments[n] + helds[n])
                            helds[n] = factors[n] * helds[n] + row
                            plains[n] = plains[n] + push * helds[n]
                            slopes[n] = slopes[n] + push * moments[n]
                    return tuple(map(tuple, (helds, moments, plains, slopes)))

                tables = (starts.at[h, 0], starts.at[h, 1], plain_sum, moment_sum)
                state = tuple(tuple(load_modes(table, v, modes)) for table in tables)
                state = lax.fori_loop(0, half // STEP, block, state)
                store_modes(plain_sum, v, modes, state[2])
                store_modes(moment_sum, v, modes, state[3])

    if chan_size > 2:
        relay(1)
    causal_states()
    if chan_size > 2:
        take_whole(1)
    causal_scan()
    for distance in range(2, chan_size - 1):
        relay(distance)
        take_whole(distance)

    last = jnp.where(place == 0, chan_size - 1, 0)
    at_end = (place == 0) | (place == chan_size - 1)

    if chan_size > 1:

        @pl.when(at_end)
        def _():
            weight_copy(last).wait()

    for h in reversed(range(HALVES)):
        if chan_size > 1:
            for part, (number, e) in enumerate(parts):
                if number == h:

                    @pl.when(at_end)
                    def _():
                        rows = pl.ds(h * half, half)
                        shard_copy(last, part, True).wait_recv()
                        multiply(
                            [(gathered.at[last, e, rows], pl.ds(e * piece, piece))], last, rows
                        )

        drive_rows(h)
        adjoint_scan(h)
        if h:
            pace(2)

            @pl.when(~at_end)
            def _():
                sum_scan(h)

            pace(3)

    def put_end(other, value):
        end_out[other] = value.astype(BF16)

    share_out(put_end, from_tiles(held_now))
    send_all(end_links)

    @pl.when(at_end)
    def _():
        sum_scan(HALVES - 1)

    held = jnp.zeros((order, width), F32)
    for block in reversed(range(ctx_size)):
        start_out[block] = held.astype(BF16)
        send_or_keep(start_links, block)
        await_slot(end_links, block)
        if block:
            held = end_in[block].astype(F32) + own_far * held
    for h in range(HALVES - 1):
        sum_scan(h)

    def put_sum(kind):
        def action(other, value):
            sums_out[other, kind] = value.astype(BF16)

        return action

    plain, slope = from_tiles(plain_sum), from_tiles(moment_sum)
    root = jnp.sqrt(2.0 * rate)
    share_out(put_sum(0), root * plain)
    share_out(put_sum(1), residues[...] * root * (0.5 * plain - rate * slope))

    send_all(sums_links)

    for other in range(ctx_size):
        await_slot(start_links, other)
        incoming[0, :, other * width : (other + 1) * width] = start_in[other].astype(F32)
    to_tiles(held_now, incoming[0])

    @pl.loop(0, across)
    def _(v):
        factors = load_modes(decay, v, every)
        terms = [
            start * factor * scale
            for start, factor, scale in zip(
                load_modes(held_now, v, every), factors, load_modes(gain, v, every)
            )
        ]

        def block(index, state):
            state = list(state)
            for step in range(STEP):
                where = (v, at(tokens - 1 - index * STEP - step))
                adjoint[where] = adjoint[where] + tree_sum(list(state))
                state = [term * factor for term, factor in zip(state, factors)]
            return tuple(state)

        lax.fori_loop(0, tokens // STEP, block, tuple(terms))

    @pl.loop(0, channels // LANES)
    def _(index):
        cols = cut(index)
        v, rows = tiled(index, 0, tokens)
        result = rounded(adjoint[v, rows, :]).T
        key_grad[cols, :] = (result * values[cols, :].astype(F32)).astype(BF16)
        value_grad[cols, :] = (result * keys[cols, :].astype(F32)).astype(BF16)

    @pl.loop(0, channels // LANES)
    def _(index):
        cols = cut(index)
        v, rows = tiled(index, 0, tokens)
        query_grad[cols, :] = (rounded(mixer[:, cols]) * conv[v, rows, :]).T.astype(BF16)

    plain = jnp.zeros((order, width), F32)
    slope = jnp.zeros((order, width), F32)
    for other in range(ctx_size):
        await_slot(sums_links, other)
        plain = plain + sums_in[other, 0].astype(F32)
        slope = slope + sums_in[other, 1].astype(F32)
    resid_grad[...] = plain
    decay_grad[...] = slope

    @pl.loop(0, ctx_size)
    def _(other):
        @pl.when(other != me)
        def _():
            for link in (causal_end_links, causal_in_links, end_links, start_links, sums_links):
                exchange(link, other).wait_send()

    for distance in range(chan_size - 1):
        for shard, present, onward, going_up in around(distance):

            @pl.when(present & onward)
            def _():
                for part in range(len(parts)):
                    if distance != paced or part >= len(parts) - 2:
                        shard_copy(shard, part, going_up, distance == 0).wait_send()


def hand_over(*refs):
    number = len(refs) // 2
    copies = [
        pltpu.make_async_copy(refs[i], refs[number + i], refs[-1].at[i]) for i in range(number)
    ]
    for copy in copies:
        copy.start()
    for copy in copies:
        copy.wait()


def local(queries, keys, values, out_grad, out_weight, residues, decay_rates):
    channels, tokens = queries.shape
    chan_size = lax.axis_size("chan")
    ctx_size = lax.axis_size("ctx")
    width = channels // ctx_size
    depth = out_grad.shape[1]
    order = residues.shape[0]
    owned = []
    if width % LANES:
        offset = lax.axis_index("ctx") * width
        owned = [lax.dynamic_slice_in_dim(x, offset, width, 1) for x in (decay_rates,)]
    number = HALVES * SPLITS
    gate = jax.ShapeDtypeStruct((channels, tokens), BF16)
    grads = jax.ShapeDtypeStruct((order, width), F32)
    shapes = (gate,) * 3 + (grads,) * 2
    vmem = pl.BlockSpec(memory_space=pltpu.VMEM)
    anywhere = pl.BlockSpec(memory_space=pl.ANY)
    dma = pltpu.SemaphoreType.DMA
    across = channels // SUB // LANES
    plane = pltpu.VMEM((tokens, channels), F32)
    tiles = pltpu.VMEM((across, tokens * SUB, LANES), F32)
    table = pltpu.VMEM((across, order * SUB, LANES), F32)
    single = pltpu.VMEM((ctx_size, order, width), BF16)
    paired = pltpu.VMEM((ctx_size, 2, order, width), BF16)
    twice = pltpu.VMEM((ctx_size, 2, order, width), F32)
    def call(*refs):
        taken = 7 + len(owned)
        body(chan_size, ctx_size, refs[:5], *refs[5:7], refs[7:taken], *refs[taken:])

    results = pl.pallas_call(
        call,
        out_shape=shapes,
        in_specs=[pl.BlockSpec(memory_space=pltpu.HBM)] * 7 + [vmem] * len(owned),
        out_specs=(vmem,) * 5,
        scratch_shapes=[
            *[pltpu.VMEM((channels, tokens), BF16)] * 3,
            *[pltpu.VMEM((order, channels), F32)] * 2,
            pltpu.VMEM((chan_size, channels, depth), BF16),
            pltpu.VMEM((chan_size, SPLITS, tokens, depth // SPLITS), BF16),
            *[plane] * 2,
            *[tiles] * 4,
            *[table] * 5,
            pltpu.VMEM((HALVES, 2, across, order * SUB, LANES), F32),
            pltpu.VMEM((2, order, channels), F32),
            *[twice] * 4,
            *[single] * 4,
            *[paired] * 2,
            dma((5 + SPLITS,)),
            dma((chan_size,)),
            dma((chan_size, number)),
            dma((chan_size, number)),
            dma((chan_size, number)),
            dma((5, ctx_size)),
            dma((5, ctx_size)),
        ],
        compiler_params=pltpu.CompilerParams(
            collective_id=0, has_side_effects=True, vmem_limit_bytes=52 * 1024 * 1024
        ),
    )(queries, keys, values, residues, decay_rates, out_grad, out_weight, *owned)
    return pl.pallas_call(
        hand_over,
        out_shape=shapes,
        in_specs=[anywhere] * 5,
        out_specs=(anywhere,) * 5,
        scratch_shapes=[dma((5,))],
        compiler_params=pltpu.CompilerParams(vmem_limit_bytes=2 * 1024 * 1024),
    )(*results)


def solution(mesh):
    placed = (
        P("chan", "ctx"),
        P("chan", "ctx"),
        P("chan", "ctx"),
        P("ctx", "chan"),
        P("chan", None),
        P(None, "chan"),
        P(None, "chan"),
    )
    return jax.shard_map(
        local,
        mesh=mesh,
        in_specs=placed,
        out_specs=(
            P("chan", "ctx"),
            P("chan", "ctx"),
            P("chan", "ctx"),
            P(None, ("chan", "ctx")),
            P(None, ("chan", "ctx")),
        ),
        check_vma=False,
    )
```

```python
import jax
import jax.numpy as jnp
from jax import lax
from jax.experimental import pallas as pl
from jax.experimental.pallas import tpu as pltpu
from jax.sharding import PartitionSpec as P

STEP = 8
SUB = 8
LANES = 128
HALVES = 2
SPLITS = 2
MESH = pl.DeviceIdType.MESH
F32, BF16 = jnp.float32, jnp.bfloat16


def rounded(x):
    return x.astype(BF16).astype(F32)


def tree_sum(terms):
    while len(terms) > 1:
        terms = [a + b for a, b in zip(terms[::2], terms[1::2])] + (
            [terms[-1]] if len(terms) % 2 else []
        )
    return terms[0]


def body(
    chan_size,
    ctx_size,
    fetched,
    out_grad,
    out_weight,
    owned,
    query_grad,
    key_grad,
    value_grad,
    resid_grad,
    decay_grad,
    queries,
    keys,
    values,
    modes,
    weight,
    gathered,
    gate,
    mixer,
    source,
    drive,
    conv,
    adjoint,
    decay,
    gain,
    held_now,
    plain_sum,
    moment_sum,
    starts,
    incoming,
    causal_end_out,
    causal_end_in,
    causal_in_out,
    causal_in_in,
    end_out,
    end_in,
    start_out,
    start_in,
    sums_out,
    sums_in,
    fetch_sems,
    weight_sems,
    shard_arrivals,
    up_sends,
    down_sends,
    sends,
    arrivals,
):
    place = lax.axis_index("chan")
    me = lax.axis_index("ctx")
    channels, tokens = queries.shape
    residues, decay_rates = modes.at[0], modes.at[1]
    depth = out_grad.shape[1]
    width = channels // ctx_size
    order = residues.shape[0]
    count = order // 8
    half = tokens // HALVES
    piece = depth // SPLITS
    own = slice(None)
    if not owned:
        own = pl.ds(pl.multiple_of(me * width, width), width)
    own_rates = owned[0] if owned else decay_rates
    tile = channels

    def links(kind, outgoing, incoming):
        return (outgoing, incoming, sends.at[kind], arrivals.at[kind])

    causal_end_links = links(0, causal_end_out, causal_end_in)
    causal_in_links = links(1, causal_in_out, causal_in_in)
    end_links = links(2, end_out, end_in)
    start_links = links(3, start_out, start_in)
    sums_links = links(4, sums_out, sums_in)

    def exchange(link, other):
        outgoing, incoming, sent, arrived = link
        return pltpu.make_async_remote_copy(
            src_ref=outgoing.at[other],
            dst_ref=incoming.at[me],
            send_sem=sent.at[other],
            recv_sem=arrived.at[me],
            device_id={"ctx": other},
            device_id_type=MESH,
        )

    def send_or_keep(link, other):
        @pl.when(other != me)
        def _():
            exchange(link, other).start()

        @pl.when(other == me)
        def _():
            link[1][me] = link[0][me]

    def await_slot(link, other):
        outgoing, incoming, sent, arrived = link

        @pl.when(other != me)
        def _():
            pltpu.make_async_remote_copy(
                src_ref=outgoing.at[other],
                dst_ref=incoming.at[other],
                send_sem=sent.at[other],
                recv_sem=arrived.at[other],
                device_id={"ctx": other},
                device_id_type=MESH,
            ).wait_recv()

    def send_all(link):
        @pl.loop(0, ctx_size)
        def _(step):
            send_or_keep(link, lax.rem(me + 1 + step, ctx_size))

    def weight_copy(shard):
        return pltpu.make_async_copy(
            out_weight.at[:, pl.ds(pl.multiple_of(shard * depth, depth), depth)],
            weight.at[shard],
            weight_sems.at[shard],
        )

    parts = [(h, e) for h in reversed(range(HALVES)) for e in range(SPLITS)]

    def shard_copy(shard, part, going_up, first=False):
        h, e = parts[part]
        rows, cols = pl.ds(h * half, half), pl.ds(e * piece, piece)
        return pltpu.make_async_remote_copy(
            src_ref=out_grad.at[rows, cols] if first else gathered.at[shard, e, rows],
            dst_ref=gathered.at[shard, e, rows],
            send_sem=(up_sends if going_up else down_sends).at[shard, part],
            recv_sem=shard_arrivals.at[shard, part],
            device_id={"chan": place + 1 if going_up else place - 1},
            device_id_type=MESH,
        )

    fetches = [
        pltpu.make_async_copy(remote, near, fetch_sems.at[i])
        for i, (remote, near) in enumerate(
            zip(fetched, (queries, keys, values, modes))
        )
    ] + [
        pltpu.make_async_copy(
            out_grad.at[:, pl.ds(e * piece, piece)], gathered.at[place, e], fetch_sems.at[4 + e]
        )
        for e in range(SPLITS)
    ]

    for fetch in fetches:
        fetch.start()
    weight_copy(place).start()
    barrier = pltpu.get_barrier_semaphore()
    for step in range(1, ctx_size):
        pl.semaphore_signal(
            barrier, inc=1, device_id={"ctx": lax.rem(me + step, ctx_size)}, device_id_type=MESH
        )
    for present, neighbour in ((place > 0, place - 1), (place < chan_size - 1, place + 1)):

        @pl.when(present)
        def _():
            pl.semaphore_signal(
                barrier, inc=1, device_id={"chan": neighbour}, device_id_type=MESH
            )

    sides = jnp.where(place > 0, 1, 0) + jnp.where(place < chan_size - 1, 1, 0)
    pl.semaphore_wait(barrier, ctx_size - 1 + sides)

    for part in range(len(parts)):

        @pl.when(place < chan_size - 1)
        def _():
            shard_copy(place, part, True, True).start()

        @pl.when(place > 0)
        def _():
            shard_copy(place, part, False, True).start()

    for fetch in fetches:
        fetch.wait()
    for distance in range(1, chan_size):
        for shard, present in (
            (place - distance, place >= distance),
            (place + distance, place + distance < chan_size),
        ):

            @pl.when(present)
            def _():
                weight_copy(shard).start()

    lanes = channels // SUB
    across = lanes // LANES

    def cut(index):
        return pl.ds(pl.multiple_of(index * LANES, LANES), LANES)

    def tiled(index, first, rows):
        return (lax.rem(index, across), pl.ds(first * SUB + index // across, rows, stride=SUB))

    def each_cut(action):
        for index in range(channels // LANES):
            action(index, slice(index * LANES, (index + 1) * LANES))

    def to_tiles(target, table):
        def action(index, cols):
            target[index % across, pl.ds(index // across, order, stride=SUB), :] = table[:, cols]

        each_cut(action)

    def from_tiles(source):
        return jnp.concatenate(
            [
                source[index % across, pl.ds(index // across, order, stride=SUB), :]
                for index in range(channels // LANES)
            ],
            axis=1,
        )

    def share_out(target, table):
        for other in range(ctx_size):
            target(other, table[:, other * width : (other + 1) * width])

    rate = decay_rates[...]
    to_tiles(decay, jnp.exp(-rate))
    to_tiles(gain, residues[...] * jnp.sqrt(2.0 * rate))

    @pl.loop(0, channels // LANES)
    def _(index):
        cols = cut(index)
        pair = keys[cols, :].astype(F32) * values[cols, :].astype(F32)
        v, rows = tiled(index, 0, tokens)
        source[v, rows, :] = pair.astype(BF16).T.astype(F32)
        gate[:, cols] = queries[cols, :].T.astype(F32)

    def mode_rows(n):
        return slice(n * SUB, (n + 1) * SUB)

    def at(token):
        return pl.ds(pl.multiple_of(token * SUB, SUB), SUB)

    def load_modes(table, v, modes):
        return [table[v, mode_rows(n), :] for n in modes]

    def store_modes(table, v, modes, state):
        for n, value in zip(modes, state):
            table[v, mode_rows(n), :] = value

    every = range(order)
    zeros = tuple(jnp.zeros((SUB, LANES), F32) for _ in every)

    @pl.loop(0, across)
    def _(v):
        factors = load_modes(decay, v, every)

        def block(index, state):
            helds, moments = map(list, state)
            for step in range(STEP):
                row = source[v, at(index * STEP + step), :]
                for n in every:
                    moments[n] = factors[n] * (moments[n] + helds[n])
                    helds[n] = factors[n] * helds[n] + row
            return tuple(helds), tuple(moments)

        state = (zeros, zeros)
        steps = half // STEP
        for h in range(HALVES):
            if h:
                for kind in range(2):
                    store_modes(starts.at[h, kind], v, every, state[kind])
            state = lax.fori_loop(h * steps, (h + 1) * steps, block, state)
        store_modes(plain_sum, v, every, state[0])
        store_modes(moment_sum, v, every, state[1])

    def put(kind):
        def action(other, value):
            causal_end_out[other, kind] = value

        return action

    share_out(put(0), from_tiles(plain_sum))
    share_out(put(1), from_tiles(moment_sum))
    send_all(causal_end_links)

    for table in (plain_sum, moment_sum, held_now):
        table[...] = jnp.zeros(table.shape, F32)

    def multiply(lefts, shard, rows, first=False):
        @pl.loop(0, channels // tile)
        def _(index):
            cols = pl.ds(pl.multiple_of(index * tile, tile), tile)
            term = tree_sum(
                [
                    lax.dot_general(
                        left[...],
                        weight[shard, cols, taken],
                        (((1,), (1,)), ((), ())),
                        preferred_element_type=F32,
                    )
                    for left, taken in lefts
                ]
            )
            mixer[rows, cols] = term if first else mixer[rows, cols] + term

    everything = slice(None)
    weight_copy(place).wait()
    multiply(
        [(gathered.at[place, e], pl.ds(e * piece, piece)) for e in range(SPLITS)],
        place,
        everything,
        True,
    )

    def around(distance):
        return (
            (place - distance, place >= distance, place < chan_size - 1, True),
            (place + distance, place + distance < chan_size, place > 0, False),
        )

    paced = chan_size - 2

    def relay(distance):
        for part in range(len(parts)):
            for shard, present, onward, going_up in around(distance):

                @pl.when(present)
                def _():
                    shard_copy(shard, part, going_up).wait_recv()

                    if distance != paced or part < 2:

                        @pl.when(onward)
                        def _():
                            shard_copy(shard, part, going_up).start()

    def pace(part):
        if paced < 1:
            return
        for shard, present, onward, going_up in around(paced):

            @pl.when(present & onward)
            def _():
                shard_copy(shard, part - 2, going_up).wait_send()
                shard_copy(shard, part, going_up).start()

    def take_whole(distance):
        for shard, present, onward, going_up in around(distance):

            @pl.when(present)
            def _():
                weight_copy(shard).wait()
                multiply(
                    [
                        (gathered.at[shard, e], pl.ds(e * piece, piece))
                        for e in range(SPLITS)
                    ],
                    shard,
                    everything,
                )

    own_rate = own_rates[:, own]
    own_far = jnp.exp(-own_rate * tokens)

    def causal_states():
        held = jnp.zeros((order, width), F32)
        moment = jnp.zeros((order, width), F32)
        for block in range(ctx_size):
            causal_in_out[block, 0] = held
            causal_in_out[block, 1] = moment
            if block < ctx_size - 1:
                await_slot(causal_end_links, block)
                moment = causal_end_in[block, 1] + own_far * (moment + float(tokens) * held)
                held = causal_end_in[block, 0] + own_far * held
        await_slot(causal_end_links, ctx_size - 1)
        send_all(causal_in_links)

    def causal_scan():
        for other in range(ctx_size):
            await_slot(causal_in_links, other)
            for kind in range(2):
                incoming[kind, :, other * width : (other + 1) * width] = causal_in_in[other, kind]
        for kind in range(2):
            to_tiles(starts.at[0, kind], incoming[kind])
        for h in range(1, HALVES):
            far = jnp.exp(-rate * float(h * half))
            plain = far * incoming[0]
            moment = far * (incoming[1] + float(h * half) * incoming[0])

            def action(index, cols):
                v, rows = index % across, pl.ds(index // across, order, stride=SUB)
                starts[h, 0, v, rows, :] = starts[h, 0, v, rows, :] + plain[:, cols]
                starts[h, 1, v, rows, :] = starts[h, 1, v, rows, :] + moment[:, cols]

            each_cut(action)

        @pl.loop(0, across)
        def _(v):
            factors = load_modes(decay, v, every)
            gains = load_modes(gain, v, every)

            def block(index, state):
                helds = list(state)
                for step in range(STEP):
                    where = (v, at(index * STEP + step))
                    row = source[where]
                    for n in every:
                        helds[n] = factors[n] * helds[n] + row
                    total = tree_sum([gains[n] * helds[n] for n in every])
                    conv[where] = rounded(total)
                return tuple(helds)

            lax.fori_loop(0, tokens // STEP, block, tuple(load_modes(starts.at[0, 0], v, every)))

    def drive_rows(h):
        @pl.loop(0, channels // LANES)
        def _(index):
            cols = cut(index)
            where = (pl.ds(h * half, half), cols)
            v, rows = tiled(index, h * half, half)
            drive[v, rows, :] = rounded(rounded(mixer[where]) * gate[where])

    def adjoint_scan(h):
        @pl.loop(0, across)
        def _(v):
            factors = load_modes(decay, v, every)
            gains = load_modes(gain, v, every)

            def block(index, state):
                helds = list(state)
                for step in range(STEP):
                    where = (v, at((h + 1) * half - 1 - index * STEP - step))
                    row = drive[where]
                    for n in every:
                        helds[n] = factors[n] * helds[n] + row
                    adjoint[where] = tree_sum([gains[n] * helds[n] for n in every])
                return tuple(helds)

            state = lax.fori_loop(0, half // STEP, block, tuple(load_modes(held_now, v, every)))
            store_modes(held_now, v, every, state)

    def sum_scan(h):
        @pl.loop(0, across)
        def _(v):
            for first in range(0, order, 8):
                modes = range(first, min(first + 8, order))
                factors = load_modes(decay, v, modes)

                def block(index, state):
                    helds, moments, plains, slopes = map(list, state)
                    for step in range(STEP):
                        where = (v, at(h * half + index * STEP + step))
                        row, push = source[where], drive[where]
                        for n in range(len(modes)):
                            moments[n] = factors[n] * (moments[n] + helds[n])
                            helds[n] = factors[n] * helds[n] + row
                            plains[n] = plains[n] + push * helds[n]
                            slopes[n] = slopes[n] + push * moments[n]
                    return tuple(map(tuple, (helds, moments, plains, slopes)))

                tables = (starts.at[h, 0], starts.at[h, 1], plain_sum, moment_sum)
                state = tuple(tuple(load_modes(table, v, modes)) for table in tables)
                state = lax.fori_loop(0, half // STEP, block, state)
                store_modes(plain_sum, v, modes, state[2])
                store_modes(moment_sum, v, modes, state[3])

    if chan_size > 2:
        relay(1)
    causal_states()
    if chan_size > 2:
        take_whole(1)
    causal_scan()
    for distance in range(2, chan_size - 1):
        relay(distance)
        take_whole(distance)

    last = jnp.where(place == 0, chan_size - 1, 0)
    at_end = (place == 0) | (place == chan_size - 1)

    if chan_size > 1:

        @pl.when(at_end)
        def _():
            weight_copy(last).wait()

    for h in reversed(range(HALVES)):
        if chan_size > 1:
            for part, (number, e) in enumerate(parts):
                if number == h:

                    @pl.when(at_end)
                    def _():
                        rows = pl.ds(h * half, half)
                        shard_copy(last, part, True).wait_recv()
                        multiply(
                            [(gathered.at[last, e, rows], pl.ds(e * piece, piece))], last, rows
                        )

        drive_rows(h)
        adjoint_scan(h)
        if h:
            pace(2)

            @pl.when(~at_end)
            def _():
                sum_scan(h)

            pace(3)

    def put_end(other, value):
        end_out[other] = value.astype(BF16)

    share_out(put_end, from_tiles(held_now))
    send_all(end_links)

    @pl.when(at_end)
    def _():
        sum_scan(HALVES - 1)

    held = jnp.zeros((order, width), F32)
    for block in reversed(range(ctx_size)):
        start_out[block] = held.astype(BF16)
        send_or_keep(start_links, block)
        await_slot(end_links, block)
        if block:
            held = end_in[block].astype(F32) + own_far * held
    for h in range(HALVES - 1):
        sum_scan(h)

    def put_sum(kind):
        def action(other, value):
            sums_out[other, kind] = value.astype(BF16)

        return action

    plain, slope = from_tiles(plain_sum), from_tiles(moment_sum)
    root = jnp.sqrt(2.0 * rate)
    share_out(put_sum(0), root * plain)
    share_out(put_sum(1), residues[...] * root * (0.5 * plain - rate * slope))

    send_all(sums_links)

    @pl.loop(0, channels // LANES)
    def _(index):
        cols = cut(index)
        v, rows = tiled(index, 0, tokens)
        query_grad[cols, :] = (rounded(mixer[:, cols]) * conv[v, rows, :]).astype(BF16).T

    for other in range(ctx_size):
        await_slot(start_links, other)
        incoming[0, :, other * width : (other + 1) * width] = start_in[other].astype(F32)
    to_tiles(held_now, incoming[0])

    @pl.loop(0, across)
    def _(v):
        factors = load_modes(decay, v, every)
        terms = [
            start * factor * scale
            for start, factor, scale in zip(
                load_modes(held_now, v, every), factors, load_modes(gain, v, every)
            )
        ]

        def block(index, state):
            state = list(state)
            for step in range(STEP):
                where = (v, at(tokens - 1 - index * STEP - step))
                adjoint[where] = adjoint[where] + tree_sum(list(state))
                state = [term * factor for term, factor in zip(state, factors)]
            return tuple(state)

        lax.fori_loop(0, tokens // STEP, block, tuple(terms))

    @pl.loop(0, channels // LANES)
    def _(index):
        cols = cut(index)
        v, rows = tiled(index, 0, tokens)
        result = adjoint[v, rows, :].astype(BF16).T.astype(F32)
        key_grad[cols, :] = (result * values[cols, :].astype(F32)).astype(BF16)
        value_grad[cols, :] = (result * keys[cols, :].astype(F32)).astype(BF16)

    plain = jnp.zeros((order, width), F32)
    slope = jnp.zeros((order, width), F32)
    for other in range(ctx_size):
        await_slot(sums_links, other)
        plain = plain + sums_in[other, 0].astype(F32)
        slope = slope + sums_in[other, 1].astype(F32)
    resid_grad[...] = plain
    decay_grad[...] = slope

    @pl.loop(0, ctx_size)
    def _(other):
        @pl.when(other != me)
        def _():
            for link in (causal_end_links, causal_in_links, end_links, start_links, sums_links):
                exchange(link, other).wait_send()

    for distance in range(chan_size - 1):
        for shard, present, onward, going_up in around(distance):

            @pl.when(present & onward)
            def _():
                for part in range(len(parts)):
                    if distance != paced or part >= len(parts) - 2:
                        shard_copy(shard, part, going_up, distance == 0).wait_send()


def hand_over(*refs):
    number = len(refs) // 2
    copies = [
        pltpu.make_async_copy(refs[i], refs[number + i], refs[-1].at[i]) for i in range(number)
    ]
    for copy in copies:
        copy.start()
    for copy in copies:
        copy.wait()


def local(queries, keys, values, out_grad, out_weight, residues, decay_rates):
    channels, tokens = queries.shape
    chan_size = lax.axis_size("chan")
    ctx_size = lax.axis_size("ctx")
    width = channels // ctx_size
    depth = out_grad.shape[1]
    order = residues.shape[0]
    owned = []
    if width % LANES:
        offset = lax.axis_index("ctx") * width
        owned = [lax.dynamic_slice_in_dim(x, offset, width, 1) for x in (decay_rates,)]
    number = HALVES * SPLITS
    gate = jax.ShapeDtypeStruct((channels, tokens), BF16)
    grads = jax.ShapeDtypeStruct((order, width), F32)
    shapes = (gate,) * 3 + (grads,) * 2
    vmem = pl.BlockSpec(memory_space=pltpu.VMEM)
    anywhere = pl.BlockSpec(memory_space=pl.ANY)
    dma = pltpu.SemaphoreType.DMA
    across = channels // SUB // LANES
    plane = pltpu.VMEM((tokens, channels), F32)
    tiles = pltpu.VMEM((across, tokens * SUB, LANES), F32)
    table = pltpu.VMEM((across, order * SUB, LANES), F32)
    single = pltpu.VMEM((ctx_size, order, width), BF16)
    paired = pltpu.VMEM((ctx_size, 2, order, width), BF16)
    twice = pltpu.VMEM((ctx_size, 2, order, width), F32)
    def call(*refs):
        taken = 6 + len(owned)
        body(chan_size, ctx_size, refs[:4], *refs[4:6], refs[6:taken], *refs[taken:])

    results = pl.pallas_call(
        call,
        out_shape=shapes,
        in_specs=[anywhere] * 6 + [vmem] * len(owned),
        out_specs=(vmem,) * 5,
        scratch_shapes=[
            *[pltpu.VMEM((channels, tokens), BF16)] * 3,
            pltpu.VMEM((2, order, channels), F32),
            pltpu.VMEM((chan_size, channels, depth), BF16),
            pltpu.VMEM((chan_size, SPLITS, tokens, depth // SPLITS), BF16),
            *[plane] * 2,
            *[tiles] * 4,
            *[table] * 5,
            pltpu.VMEM((HALVES, 2, across, order * SUB, LANES), F32),
            pltpu.VMEM((2, order, channels), F32),
            *[twice] * 4,
            *[single] * 4,
            *[paired] * 2,
            dma((4 + SPLITS,)),
            dma((chan_size,)),
            dma((chan_size, number)),
            dma((chan_size, number)),
            dma((chan_size, number)),
            dma((5, ctx_size)),
            dma((5, ctx_size)),
        ],
        compiler_params=pltpu.CompilerParams(
            collective_id=0, has_side_effects=True, vmem_limit_bytes=52 * 1024 * 1024
        ),
    )(queries, keys, values, jnp.stack([residues, decay_rates]), out_grad, out_weight, *owned)
    return pl.pallas_call(
        hand_over,
        out_shape=shapes,
        in_specs=[anywhere] * 5,
        out_specs=(anywhere,) * 5,
        scratch_shapes=[dma((5,))],
        compiler_params=pltpu.CompilerParams(vmem_limit_bytes=2 * 1024 * 1024),
    )(*results)


def solution(mesh):
    placed = (
        P("chan", "ctx"),
        P("chan", "ctx"),
        P("chan", "ctx"),
        P("ctx", "chan"),
        P("chan", None),
        P(None, "chan"),
        P(None, "chan"),
    )
    return jax.shard_map(
        local,
        mesh=mesh,
        in_specs=placed,
        out_specs=(
            P("chan", "ctx"),
            P("chan", "ctx"),
            P("chan", "ctx"),
            P(None, ("chan", "ctx")),
            P(None, ("chan", "ctx")),
        ),
        check_vma=False,
    )
```
